256 devices in a mesh: freq: 8 (over z_lo, core), col: 32 (over x, y, z_hi).
Axes of the slice: x: 4, y: 4, z: 8 (z_hi: 2, z_lo: 4; z = z_hi * 4 + z_lo), core: 2. Of those that a mesh axis runs over, the one named last changes fastest.
Arguments:
- spectra: bfloat16 [2, 16, 4096, 4096], P(None, None, 'freq', 'col'), may hold values from -0.62890625 to 0.62890625
- wavelet: float32 [2, 16], P(None, 'freq'), may hold values from -1.5 to 1.5
Outputs:
- predicted: bfloat16 [2, 16, 384, 4096], P(None, 'freq', None, 'col')
The draws below stay inside these ranges and needn't reach their ends.
All inputs are finite; a program needn't handle non-finite values.
Results may differ from the reference program's by a relative error of at most 0.001.
Values may be sent and summed in bfloat16 or wider, within the bound.
No kernel may reach another device: no remote copies, remote signals or barrier semaphores. Data moves between devices by JAX's collectives and lax.ppermute only.
A program may use at most 128 MiB of HBM per device.

```python
import jax
import jax.numpy as jnp
from jax import lax

NS = 4096
NOUT = 384
NF = 16


def shard_levels(rng, extent, cuts, least, high):
    level, own = 1.0, jax.random.fold_in(rng, 6)
    for dim, blocks in cuts:
        steps = jnp.exp(jax.random.uniform(jax.random.fold_in(own, dim), (blocks,), jnp.float32, least / len(cuts), high / len(cuts)))
        level = level * jnp.repeat(steps, extent[dim] // blocks).reshape([-1 if axis == dim else 1 for axis in range(len(extent))])
    return level


def scatter_about(own_key, dims, scale, limit, pieces=(), dtype=jnp.bfloat16):
    factor_of = shard_levels(own_key, dims, pieces, -0.22, 0.18) if pieces else 1.0
    values = jax.random.normal(own_key, dims, jnp.float32) * scale * factor_of
    return jnp.minimum(jnp.maximum(values, -limit), limit).astype(dtype)


def setup_inputs(seed: int = 0) -> dict:
    streams_of = jax.random.split(jax.random.key(seed), 3)
    return {
        "spectra": scatter_about(streams_of[0], (2, NF, NS, NS), 0.105, 0.62890625, ((2, 8), (3, 32))),
        "wavelet": jnp.clip(jax.random.uniform(streams_of[1], (2, NF), jnp.float32, -1.5, 1.5) * shard_levels(streams_of[1], (2, NF), ((1, 8),), -0.4, 0.0), -1.5, 1.5),
    }


def matmul_full(left, right):
    return jnp.dot(left.astype(jnp.float32), right.astype(jnp.float32), precision=lax.Precision.HIGHEST)


def single_frequency(slab):
    upper = slab[:, :NOUT, :]
    real_part = matmul_full(upper[0], slab[0]) - matmul_full(upper[1], slab[1])
    imag_part = matmul_full(upper[0], slab[1]) + matmul_full(upper[1], slab[0])
    return jnp.stack([real_part, imag_part])


def reference(spectra, wavelet):
    ordered = jnp.moveaxis(spectra, 1, 0)
    products = lax.map(single_frequency, ordered)
    products = jnp.moveaxis(products, 0, 1)
    wave_real = wavelet[0][:, None, None]
    wave_imag = wavelet[1][:, None, None]
    real_out = -(wave_real * products[0] - wave_imag * products[1])
    imag_out = -(wave_real * products[1] + wave_imag * products[0])
    return jnp.stack([real_out, imag_out]).astype(jnp.bfloat16)
```

```python
import jax
import jax.numpy as jnp
from jax import lax
from jax.sharding import Mesh, PartitionSpec as P

NOUT = 384
AXES = ("zq", "zr", "core", "x", "y", "zh")
SIZES = (2, 2, 2, 4, 4, 2)


def coordinates():
    out = [()]
    for size in SIZES:
        out = [c + (i,) for c in out for i in range(size)]
    return out


def flat(c):
    index = 0
    for i, size in zip(c, SIZES):
        index = index * size + i
    return index


def moved(target):
    pairs = []
    for c in coordinates():
        t = target(*c)
        if t is not None and tuple(t) != c:
            pairs.append((flat(c), flat(t)))
    return pairs


def send(value, target):
    return lax.ppermute(value, AXES, moved(target))


def home(zq, zr, core, x, y, zh):
    return (x // 2, zr, x % 2, 2 * zq + core, y, zh)


def local(spectra, wavelet):
    zq, zr, core = lax.axis_index("zq"), lax.axis_index("zr"), lax.axis_index("core")
    y, zh = lax.axis_index("y"), lax.axis_index("zh")
    window = NOUT * spectra.shape[2] // 512
    lanes = spectra.shape[3]

    back = [(b, a) for a, b in moved(home)]
    stay = (zq == lax.axis_index("x") // 2) & (core == lax.axis_index("x") % 2)
    wave = jnp.where(stay, wavelet, lax.ppermute(wavelet, AXES, back))

    parted = spectra.reshape((2, 2, 2, 2, 2) + spectra.shape[2:])
    parted = parted.transpose(4, 1, 3, 2, 0, 5, 6).reshape((2, 8, 2) + spectra.shape[2:])

    def exchange(block):
        return lax.all_to_all(block, ("x", "zr"), split_axis=0, concat_axis=0, tiled=True)

    upper = [exchange(parted[g, :, :, :window]) for g in range(2)]
    lower = exchange(parted[:, :, :, window:].transpose(1, 0, 2, 3, 4))

    outs = []
    for g in range(2):
        shots = upper[g].reshape((4, 2) + upper[g].shape[1:])[:, 0]
        near, far = shots[:2], shots[2:]
        source = (zq == 0) & (core == 0)
        here = source & (y < 2)
        own = jnp.where(here, near, 0) + send(
            near, lambda q, r, c, x, y, h: (0, r, y // 2, x, y, h) if q == 0 and c == 0 and y >= 2 else None
        ) + send(far, lambda q, r, c, x, y, h: (1, r, y // 2, x, y, h) if q == 0 and c == 0 else None)
        other = send(
            near, lambda q, r, c, x, y, h: (0, r, y // 2, x, y, 1 - h) if q == 0 and c == 0 else None
        ) + send(far, lambda q, r, c, x, y, h: (1, r, y // 2, x, y, 1 - h) if q == 0 and c == 0 else None)
        pieces = []
        for piece in (own, other):
            turned = [piece] + [
                send(piece, lambda q, r, c, x, y, h: (q, r, c, x, (y + s) % 4, h) if y // 2 == c else None)
                for s in (1, 2, 3)
            ]
            pieces.append(
                [
                    lax.select_n((y - 2 * core - low) % 4, *turned)
                    for low in range(2)
                ]
            )
        blocks = []
        for low in range(2):
            a, b = pieces[0][low], pieces[1][low]
            blocks.append(jnp.where(zh == 0, a, b))
            blocks.append(jnp.where(zh == 0, b, a))
        left = jnp.stack(blocks, 1)
        right = jnp.concatenate([upper[g], lower[:, g]], 2).reshape(4, 2, 2, 4, lanes, lanes)

        def dot(i, j):
            return jnp.einsum(
                "rbmk,xrbkc->xmc", left[:, :, i], right[:, :, j], preferred_element_type=jnp.float32
            )

        partial = jnp.stack([dot(0, 0) - dot(1, 1), dot(0, 1) + dot(1, 0)], 1)
        partial = partial.reshape((2, 2) + partial.shape[1:])
        even, odd = partial[:, 0], partial[:, 1]
        kept = jnp.where(core == 0, even, odd) + send(
            jnp.where(core == 0, odd, even), lambda q, r, c, x, y, h: (q, r, 1 - c, x, y, h)
        )
        product = jnp.where(zq == 0, kept[0], kept[1]) + send(
            jnp.where(zq == 0, kept[1], kept[0]), lambda q, r, c, x, y, h: (1 - q, r, c, x, y, h)
        )
        real_out = -(wave[0, g] * product[0] - wave[1, g] * product[1])
        imag_out = -(wave[0, g] * product[1] + wave[1, g] * product[0])
        done = jnp.stack([real_out, imag_out]).astype(jnp.bfloat16)
        outs.append(jnp.where(stay, done, send(done, home)))
    return jnp.stack(outs, 1)


def solution(mesh):
    fine = Mesh(mesh.devices.reshape(SIZES), AXES)
    freq, col = AXES[:3], AXES[3:]
    return jax.shard_map(
        local,
        mesh=fine,
        in_specs=(P(None, None, freq, col), P(None, freq)),
        out_specs=P(None, freq, None, col),
        check_vma=False,
    )
```

```python
import jax
import jax.numpy as jnp
from jax import lax
from jax.experimental import pallas as pl
from jax.experimental.pallas import tpu as pltpu
from jax.sharding import Mesh, PartitionSpec as P

NOUT = 384
AXES = ("zq", "zr", "core", "x", "y", "zh")
SIZES = (2, 2, 2, 4, 4, 2)


def coordinates():
    out = [()]
    for size in SIZES:
        out = [c + (i,) for c in out for i in range(size)]
    return out


def flat(c):
    index = 0
    for i, size in zip(c, SIZES):
        index = index * size + i
    return index


def moved(target):
    pairs = []
    for c in coordinates():
        t = target(*c)
        if t is not None:
            pairs.append((flat(c), flat(t)))
    return pairs


def send(value, target):
    return lax.ppermute(value, AXES, moved(target))


def swap_core(value):
    return lax.ppermute(value, "core", [(0, 1), (1, 0)])


def contract(place, shots, a_own, a_peer, b_own, b_peer):
    half, lanes = shots.shape[-2:]
    depth = 16 * lanes

    def kernel(place_ref, u_ref, ao_ref, ap_ref, bo_ref, bp_ref, sent_ref, kept_ref, left):
        core, zh, zq = place_ref[0], place_ref[1], place_ref[2]
        for xl in range(2):
            for ys in range(4):
                for zs in range(2):
                    start = ((xl * 4 + ys) * 2 + zs) * lanes
                    for part in range(2):
                        left[part * half : (part + 1) * half, start : start + lanes] = u_ref[ys, zs ^ zh, xl, part]

        first = core == 0
        for side, out in ((1, sent_ref), (0, kept_ref)):
            for low in range(2):
                x = 2 * (zq ^ side) + low
                rows = []
                for zr in range(2):
                    i = 2 * x + zr
                    parts = []
                    for part in range(2):
                        ao, ap, bo, bp = ao_ref[i, part], ap_ref[i, part], bo_ref[i, part], bp_ref[i, part]
                        parts.append(
                            jnp.concatenate(
                                [
                                    jnp.where(first, ao, ap),
                                    jnp.where(first, ap, ao),
                                    jnp.where(first, bo, bp),
                                    jnp.where(first, bp, bo),
                                ],
                                0,
                            )
                        )
                    rows.append(jnp.concatenate(parts, 1))
                right = jnp.concatenate(rows, 0)
                both = jnp.dot(left[...], right, preferred_element_type=jnp.float32)
                out[low, 0] = both[:half, :lanes] - both[half:, lanes:]
                out[low, 1] = both[:half, lanes:] + both[half:, :lanes]

    vmem = pl.BlockSpec(memory_space=pltpu.VMEM)
    result = jax.ShapeDtypeStruct((2, 2, half, lanes), jnp.float32)
    return pl.pallas_call(
        kernel,
        out_shape=(result, result),
        in_specs=[pl.BlockSpec(memory_space=pltpu.SMEM)] + [vmem] * 5,
        out_specs=(vmem, vmem),
        scratch_shapes=[pltpu.VMEM((2 * half, depth), jnp.bfloat16)],
        cost_estimate=pl.CostEstimate(
            flops=2 * 2 * half * depth * 8 * lanes, bytes_accessed=7 << 20, transcendentals=0
        ),
        compiler_params=pltpu.CompilerParams(vmem_limit_bytes=40 << 20),
    )(place, shots, a_own, a_peer, b_own, b_peer)


def local(spectra, wavelet):
    zq, core, x = lax.axis_index("zq"), lax.axis_index("core"), lax.axis_index("x")
    zh = lax.axis_index("zh")
    place = jnp.stack([core, zh, zq]).astype(jnp.int32)
    rows, lanes = spectra.shape[2:]
    window = NOUT * rows // 512
    half = window // 2
    first = core == 0

    wave = send(wavelet, lambda q, r, c, x, y, h: (x // 2, r, x % 2, 2 * q + c, y, h))

    def ordered(block):
        block = block.reshape((2, 2, 2, 2, 2) + block.shape[2:])
        return block.transpose(4, 1, 3, 2, 0, 5, 6).reshape((2, 8, 2) + block.shape[5:])

    low, mid, rest = spectra[:, :, :half], spectra[:, :, half:window], spectra[:, :, window:]
    passed = swap_core(jnp.where(first, mid, low))
    a = ordered(jnp.where(first, low, passed))
    b = ordered(
        jnp.where(first, jnp.concatenate([rest, passed], 2), spectra[:, :, half:])
    )

    def exchange(block):
        return lax.all_to_all(block, ("x", "zr"), split_axis=0, concat_axis=0, tiled=True)

    a_own = [exchange(a[g]) for g in range(2)]
    b_own = [exchange(b[g]) for g in range(2)]

    outs = []
    for g in range(2):
        shots = a_own[g].reshape((4, 2) + a_own[g].shape[1:])[:, 0]
        near, far = shots[:2], shots[2:]
        own = jnp.where(zq == 0, near, send(far, lambda q, r, c, x, y, h: (1, r, c, x, y, h) if q == 0 else None))
        other = send(near, lambda q, r, c, x, y, h: (0, r, c, x, y, 1 - h) if q == 0 else None) + send(
            far, lambda q, r, c, x, y, h: (1, r, c, x, y, 1 - h) if q == 0 else None
        )
        pieces = jnp.stack([own, other])
        pieces = jnp.broadcast_to(pieces[None], (4,) + pieces.shape)
        spread = lax.all_to_all(pieces, "y", split_axis=0, concat_axis=0, tiled=True)
        a_peer, b_peer = swap_core(a_own[g]), swap_core(b_own[g])
        sent, kept = contract(place, spread, a_own[g], a_peer, b_own[g], b_peer)
        product = kept + send(sent, lambda q, r, c, x, y, h: (1 - q, r, c, x, y, h))
        real_out = -(wave[0, g] * product[:, 0] - wave[1, g] * product[:, 1])
        imag_out = -(wave[0, g] * product[:, 1] + wave[1, g] * product[:, 0])
        done = jnp.stack([real_out, imag_out], 1).astype(jnp.bfloat16)
        same, cross = jnp.where(first, done[0], done[1]), jnp.where(first, done[1], done[0])
        same = send(same, lambda q, r, c, x, y, h: (x // 2, r, x % 2, 2 * q + c, y, h))
        cross = send(cross, lambda q, r, c, x, y, h: (x // 2, r, x % 2, 2 * q + 1 - c, y, h))
        even = x % 2 == 0
        outs.append(
            jnp.concatenate([jnp.where(even, same, cross), jnp.where(even, cross, same)], 1)
        )
    return jnp.stack(outs, 1)


def solution(mesh):
    fine = Mesh(mesh.devices.reshape(SIZES), AXES)
    freq, col = AXES[:3], AXES[3:]
    return jax.shard_map(
        local,
        mesh=fine,
        in_specs=(P(None, None, freq, col), P(None, freq)),
        out_specs=P(None, freq, None, col),
        check_vma=False,
    )
```

```python
import jax
import jax.numpy as jnp
from jax import lax
from jax.experimental import pallas as pl
from jax.experimental.pallas import tpu as pltpu
from jax.sharding import Mesh, PartitionSpec as P


NOUT = 384
AXES = ("zq", "zr", "core", "x", "y", "zh")
SIZES = (2, 2, 2, 4, 4, 2)


def coordinates():
    out = [()]
    for size in SIZES:
        out = [c + (i,) for c in out for i in range(size)]
    return out


def flat(c):
    index = 0
    for i, size in zip(c, SIZES):
        index = index * size + i
    return index


def moved(target):
    pairs = []
    for c in coordinates():
        t = target(*c)
        if t is not None:
            pairs.append((flat(c), flat(t)))
    return pairs


def send(value, target):
    return lax.ppermute(value, AXES, moved(target))


def swap_core(value):
    return lax.ppermute(value, "core", [(0, 1), (1, 0)])


def contract(g, place, turned, a_own, a_peer, b_own, b_peer):
    half, lanes = turned[0].shape[-2:]
    depth = 16 * lanes

    def kernel(place_ref, u0, u1, u2, u3, ao_ref, ap_ref, bo_ref, bp_ref, sent_ref, kept_ref, left):
        core, zh, zq, y = place_ref[0], place_ref[1], place_ref[2], place_ref[3]
        for step, u_ref in enumerate((u0, u1, u2, u3)):
            ys = (y + 4 - step) % 4
            for xl in range(2):
                for piece in range(2):
                    start = pl.multiple_of(((xl * 4 + ys) * 2 + (piece ^ zh)) * lanes, lanes)
                    for part in range(2):
                        left[part * half : (part + 1) * half, pl.ds(start, lanes)] = u_ref[piece, xl, part]

        first = core == 0
        for side, out in ((1, sent_ref), (0, kept_ref)):
            for low in range(2):
                x = 2 * (zq ^ side) + low
                rows = []
                for zr in range(2):
                    i = 2 * x + zr
                    parts = []
                    for part in range(2):
                        ao, ap = ao_ref[i, g, part], ap_ref[i, g, part]
                        bo, bp = bo_ref[i, part], bp_ref[i, part]
                        parts.append(
                            jnp.concatenate(
                                [
                                    jnp.where(first, ao, ap),
                                    jnp.where(first, ap, ao),
                                    jnp.where(first, bo, bp),
                                    jnp.where(first, bp, bo),
                                ],
                                0,
                            )
                        )
                    rows.append(jnp.concatenate(parts, 1))
                right = jnp.concatenate(rows, 0)
                both = jnp.dot(left[...], right, preferred_element_type=jnp.float32)
                out[low, 0] = both[:half, :lanes] - both[half:, lanes:]
                out[low, 1] = both[:half, lanes:] + both[half:, :lanes]

    vmem = pl.BlockSpec(memory_space=pltpu.VMEM)
    result = jax.ShapeDtypeStruct((2, 2, half, lanes), jnp.float32)
    return pl.pallas_call(
        kernel,
        out_shape=(result, result),
        in_specs=[pl.BlockSpec(memory_space=pltpu.SMEM)] + [vmem] * 8,
        out_specs=(vmem, vmem),
        scratch_shapes=[pltpu.VMEM((2 * half, depth), jnp.bfloat16)],
        cost_estimate=pl.CostEstimate(
            flops=2 * 2 * half * depth * 8 * lanes, bytes_accessed=7 << 20, transcendentals=0
        ),
        compiler_params=pltpu.CompilerParams(vmem_limit_bytes=40 << 20),
    )(place, *turned, a_own, a_peer, b_own, b_peer)


def step(spectra, wavelet):
    zq, core, x = lax.axis_index("zq"), lax.axis_index("core"), lax.axis_index("x")
    y, zh = lax.axis_index("y"), lax.axis_index("zh")
    place = jnp.stack([core, zh, zq, y]).astype(jnp.int32)
    rows, _ = spectra.shape[2:]
    window = NOUT * rows // 512
    half = window // 2
    first = core == 0

    wave = send(wavelet, lambda q, r, c, x, y, h: (x // 2, r, x % 2, 2 * q + c, y, h))

    def ordered(block):
        return block.reshape((2, 2, 2, 2, 2) + block.shape[2:])

    low, mid, rest = spectra[:, :, :half], spectra[:, :, half:window], spectra[:, :, window:]
    passed = swap_core(jnp.where(first, mid, low))
    a = ordered(jnp.where(first, low, passed)).transpose(1, 3, 2, 4, 0, 5, 6)
    a = a.reshape((8, 2, 2) + a.shape[5:])
    b = ordered(
        jnp.where(first, jnp.concatenate([rest, passed], 2), spectra[:, :, half:])
    ).transpose(4, 1, 3, 2, 0, 5, 6)
    b = b.reshape((2, 8, 2) + b.shape[5:])

    def exchange(block):
        return lax.all_to_all(block, ("x", "zr"), split_axis=0, concat_axis=0, tiled=True)

    a_own = exchange(a)
    a_own, b = lax.optimization_barrier((a_own, b))
    a_peer = swap_core(a_own)
    b_own, b_peer = [], []
    for g in range(2):
        b_own.append(exchange(b[g]))
        b_peer.append(swap_core(b_own[g]))

    outs = []
    for g in range(2):
        shots = a_own.reshape((4, 2) + a_own.shape[1:])[:, 0, g]
        near, far = shots[:2], shots[2:]
        across = send(near, lambda q, r, c, x, y, h: (0, r, c, x, y, 1 - h) if q == 0 else None)
        up = send(far, lambda q, r, c, x, y, h: (1, r, c, x, y, h) if q == 0 else None)
        down = send(far, lambda q, r, c, x, y, h: (1, r, c, x, y, 1 - h) if q == 0 else None)
        near, across, up, down = lax.optimization_barrier((near, across, up, down))
        pieces = jnp.stack([jnp.where(zq == 0, near, up), jnp.where(zq == 0, across, down)])
        turned = [pieces] + [
            lax.ppermute(pieces, "y", [(i, (i + s) % 4) for i in range(4)]) for s in (1, 3, 2)
        ]
        turned = [turned[0], turned[1], turned[3], turned[2]]
        sent, kept = contract(g, place, turned, a_own, a_peer, b_own[g], b_peer[g])
        product = kept + send(sent, lambda q, r, c, x, y, h: (1 - q, r, c, x, y, h))
        real_out = -(wave[0, g] * product[:, 0] - wave[1, g] * product[:, 1])
        imag_out = -(wave[0, g] * product[:, 1] + wave[1, g] * product[:, 0])
        done = jnp.stack([real_out, imag_out], 1).astype(jnp.bfloat16)
        same, cross = jnp.where(first, done[0], done[1]), jnp.where(first, done[1], done[0])
        same = send(same, lambda q, r, c, x, y, h: (x // 2, r, x % 2, 2 * q + c, y, h))
        cross = send(cross, lambda q, r, c, x, y, h: (x // 2, r, x % 2, 2 * q + 1 - c, y, h))
        even = x % 2 == 0
        outs.append(
            jnp.concatenate([jnp.where(even, same, cross), jnp.where(even, cross, same)], 1)
        )
    return jnp.stack(outs, 1)


def solution(mesh):
    fine = Mesh(mesh.devices.reshape(SIZES), AXES)
    freq, col = AXES[:3], AXES[3:]
    return jax.shard_map(
        step,
        mesh=fine,
        in_specs=(P(None, None, freq, col), P(None, freq)),
        out_specs=P(None, freq, None, col),
        check_vma=False,
    )
```

```python
import jax
import jax.numpy as jnp
from jax import lax
from jax.experimental import pallas as pl
from jax.experimental.pallas import tpu as pltpu
from jax.sharding import Mesh, PartitionSpec as P


NOUT = 384
AXES = ("zq", "zr", "core", "x", "yq", "yr", "zh")
SIZES = (2, 2, 2, 4, 2, 2, 2)


def coordinates():
    out = [()]
    for size in SIZES:
        out = [c + (i,) for c in out for i in range(size)]
    return out


def flat(c):
    index = 0
    for i, size in zip(c, SIZES):
        index = index * size + i
    return index


def moved(target):
    pairs = []
    for c in coordinates():
        t = target(*c)
        if t is not None:
            pairs.append((flat(c), flat(t)))
    return pairs


def send(value, target):
    return lax.ppermute(value, AXES, moved(target))


def swap_core(value):
    return lax.ppermute(value, "core", [(0, 1), (1, 0)])


def contract(turn, place, mine, theirs, a_own, a_peer, b_own, b_peer):
    half, lanes = mine[0].shape[-2:]
    depth = 16 * lanes

    def kernel(place_ref, m0, m1, t0, t1, ao_ref, ap_ref, bo_ref, bp_ref, sent_ref, kept_ref, left):
        core, zh, zq, yq, yr = (place_ref[i] for i in range(5))
        for far, refs in enumerate(((m0, m1), (t0, t1))):
            for piece, u_ref in enumerate(refs):
                for xl in range(2):
                    for yl in range(2):
                        block = (xl * 4 + 2 * (yq ^ far) + yl) * 2 + (piece ^ zh)
                        start = pl.multiple_of(block * lanes, lanes)
                        for part in range(2):
                            left[part * half : (part + 1) * half, pl.ds(start, lanes)] = u_ref[xl, yl, part]

        first = core == 0
        for side, out in ((1, sent_ref), (0, kept_ref)):
            for low in range(2):
                x = 2 * (zq ^ side) + low
                rows = []
                for zr in range(2):
                    i = 4 * x + 2 * (yr ^ turn) + zr
                    parts = []
                    for part in range(2):
                        ao, ap = ao_ref[i, part], ap_ref[i, part]
                        bo, bp = bo_ref[i, part], bp_ref[i, part]
                        parts.append(
                            jnp.concatenate(
                                [
                                    jnp.where(first, ao, ap),
                                    jnp.where(first, ap, ao),
                                    jnp.where(first, bo, bp),
                                    jnp.where(first, bp, bo),
                                ],
                                0,
                            )
                        )
                    rows.append(jnp.concatenate(parts, 1))
                right = jnp.concatenate(rows, 0)
                both = jnp.dot(left[...], right, preferred_element_type=jnp.float32)
                out[low, 0] = both[:half, :lanes] - both[half:, lanes:]
                out[low, 1] = both[:half, lanes:] + both[half:, :lanes]

    vmem = pl.BlockSpec(memory_space=pltpu.VMEM)
    result = jax.ShapeDtypeStruct((2, 2, half, lanes), jnp.float32)
    return pl.pallas_call(
        kernel,
        out_shape=(result, result),
        in_specs=[pl.BlockSpec(memory_space=pltpu.SMEM)] + [vmem] * 8,
        out_specs=(vmem, vmem),
        scratch_shapes=[pltpu.VMEM((2 * half, depth), jnp.bfloat16)],
        cost_estimate=pl.CostEstimate(
            flops=2 * 2 * half * depth * 8 * lanes, bytes_accessed=7 << 20, transcendentals=0
        ),
        compiler_params=pltpu.CompilerParams(vmem_limit_bytes=40 << 20),
    )(place, *mine, *theirs, a_own, a_peer, b_own, b_peer)


def step(spectra, wavelet):
    zq, core, x = lax.axis_index("zq"), lax.axis_index("core"), lax.axis_index("x")
    yq, yr, zh = lax.axis_index("yq"), lax.axis_index("yr"), lax.axis_index("zh")
    place = jnp.stack([core, zh, zq, yq, yr]).astype(jnp.int32)
    rows, _ = spectra.shape[2:]
    window = NOUT * rows // 512
    half = window // 2
    first = core == 0

    wave = send(wavelet, lambda q, r, c, x, a, b, h: (x // 2, r, x % 2, 2 * q + c, a, b, h))
    wave = jnp.where(yr == 0, wave[:, 0], wave[:, 1])

    def ordered(block):
        block = block.reshape((2, 2, 2, 2, 2) + block.shape[2:])
        return block.transpose(1, 3, 4, 2, 0, 5, 6).reshape((16, 2) + block.shape[5:])

    low, mid, rest = spectra[:, :, :half], spectra[:, :, half:window], spectra[:, :, window:]
    passed = swap_core(jnp.where(first, mid, low))
    a = ordered(jnp.where(first, low, passed))
    b = ordered(jnp.where(first, jnp.concatenate([rest, passed], 2), spectra[:, :, half:]))

    def exchange(block):
        return lax.all_to_all(block, ("x", "yr", "zr"), split_axis=0, concat_axis=0, tiled=True)

    a_own = exchange(a)
    a_own, b = lax.optimization_barrier((a_own, b))
    b_own = exchange(b)
    a_peer = swap_core(a_own)
    b_peer = swap_core(b_own)

    shots = a_own.reshape((4, 2, 2) + a_own.shape[1:])[:, :, 0]
    near, far = shots[:2], shots[2:]
    up = send(far, lambda q, r, c, x, a, b, h: (1, r, c, x, a, b, h) if q == 0 else None)
    across = send(near, lambda q, r, c, x, a, b, h: (0, r, c, x, a, b, 1 - h) if q == 0 else None)
    down = send(far, lambda q, r, c, x, a, b, h: (1, r, c, x, a, b, 1 - h) if q == 0 else None)
    mine = [jnp.where(zq == 0, near, up), jnp.where(zq == 0, across, down)]
    theirs = [lax.ppermute(piece, "yq", [(0, 1), (1, 0)]) for piece in mine]

    def homeward(turn, same, cross):
        same = send(
            same, lambda q, r, c, x, a, b, h: (x // 2, r, x % 2, 2 * q + c, a, b ^ turn, h)
        )
        cross = send(
            cross, lambda q, r, c, x, a, b, h: (x // 2, r, x % 2, 2 * q + 1 - c, a, b ^ turn, h)
        )
        even = x % 2 == 0
        same, cross = jnp.where(even, same, cross), jnp.where(even, cross, same)
        return jnp.concatenate([same, cross], 1)

    arrived = []
    for turn in range(2):
        sent, kept = contract(turn, place, mine, theirs, a_own, a_peer, b_own, b_peer)
        other = send(sent, lambda q, r, c, x, a, b, h: (1 - q, r, c, x, a, b, h))
        if turn:
            other, kept, early = lax.optimization_barrier((other, kept, homeward(0, same, cross)))
            arrived.append(early)
        product = kept + lax.optimization_barrier(other)
        real_out = -(wave[0] * product[:, 0] - wave[1] * product[:, 1])
        imag_out = -(wave[0] * product[:, 1] + wave[1] * product[:, 0])
        done = jnp.stack([real_out, imag_out], 1).astype(jnp.bfloat16)
        same, cross = jnp.where(first, done[0], done[1]), jnp.where(first, done[1], done[0])
        same, cross = lax.optimization_barrier((same, cross))
    arrived.append(homeward(1, same, cross))
    return jnp.stack(
        [jnp.where(yr == 0, arrived[0], arrived[1]), jnp.where(yr == 0, arrived[1], arrived[0])], 1
    )


def solution(mesh):
    fine = Mesh(mesh.devices.reshape(SIZES), AXES)
    freq, col = AXES[:3], AXES[3:]
    return jax.shard_map(
        step,
        mesh=fine,
        in_specs=(P(None, None, freq, col), P(None, freq)),
        out_specs=P(None, freq, None, col),
        check_vma=False,
    )
```

```python
import jax
import jax.numpy as jnp
from jax import lax
from jax.experimental import pallas as pl
from jax.experimental.pallas import tpu as pltpu
from jax.sharding import Mesh, PartitionSpec as P


NOUT = 384
AXES = ("zq", "zr", "core", "x", "y", "zh")
SIZES = (2, 2, 2, 4, 4, 2)


def coordinates():
    out = [()]
    for size in SIZES:
        out = [c + (i,) for c in out for i in range(size)]
    return out


def flat(c):
    index = 0
    for i, size in zip(c, SIZES):
        index = index * size + i
    return index


def moved(target):
    pairs = []
    for c in coordinates():
        t = target(*c)
        if t is not None:
            pairs.append((flat(c), flat(t)))
    return pairs


def send(value, target):
    return lax.ppermute(value, AXES, moved(target))


def swap_core(value):
    return lax.ppermute(value, "core", [(0, 1), (1, 0)])


def contract(g, place, turned, a_own, a_peer, b_own, b_peer):
    half, lanes = turned[0].shape[-2:]
    depth = 16 * lanes

    def kernel(place_ref, u0, u1, u2, u3, ao_ref, ap_ref, bo_ref, bp_ref, o0, o1, o2, o3, left):
        core, zh, zq, y = place_ref[0], place_ref[1], place_ref[2], place_ref[3]
        for step, u_ref in enumerate((u0, u1, u2, u3)):
            ys = (y + 4 - step) % 4
            for xl in range(2):
                for piece in range(2):
                    start = pl.multiple_of(((xl * 4 + ys) * 2 + (piece ^ zh)) * lanes, lanes)
                    for part in range(2):
                        left[part * half : (part + 1) * half, pl.ds(start, lanes)] = u_ref[piece, xl, part]

        first = core == 0
        for t, out in enumerate((o0, o1, o2, o3)):
            x = (2 * zq + core) ^ t
            rows = []
            for zr in range(2):
                i = 2 * x + zr
                parts = []
                for part in range(2):
                    ao, ap = ao_ref[i, g, part], ap_ref[i, g, part]
                    bo, bp = bo_ref[i, part], bp_ref[i, part]
                    parts.append(
                        jnp.concatenate(
                            [
                                jnp.where(first, ao, ap),
                                jnp.where(first, ap, ao),
                                jnp.where(first, bo, bp),
                                jnp.where(first, bp, bo),
                            ],
                            0,
                        )
                    )
                rows.append(jnp.concatenate(parts, 1))
            right = jnp.concatenate(rows, 0)
            both = jnp.dot(left[...], right, preferred_element_type=jnp.float32)
            out[0] = both[:half, :lanes] - both[half:, lanes:]
            out[1] = both[:half, lanes:] + both[half:, :lanes]

    vmem = pl.BlockSpec(memory_space=pltpu.VMEM)
    result = jax.ShapeDtypeStruct((2, half, lanes), jnp.float32)
    return pl.pallas_call(
        kernel,
        out_shape=(result,) * 4,
        in_specs=[pl.BlockSpec(memory_space=pltpu.SMEM)] + [vmem] * 8,
        out_specs=(vmem,) * 4,
        scratch_shapes=[pltpu.VMEM((2 * half, depth), jnp.bfloat16)],
        cost_estimate=pl.CostEstimate(
            flops=2 * 2 * half * depth * 8 * lanes, bytes_accessed=7 << 20, transcendentals=0
        ),
        compiler_params=pltpu.CompilerParams(vmem_limit_bytes=40 << 20),
    )(place, *turned, a_own, a_peer, b_own, b_peer)


def step(spectra, wavelet):
    zq, core, x = lax.axis_index("zq"), lax.axis_index("core"), lax.axis_index("x")
    y, zh = lax.axis_index("y"), lax.axis_index("zh")
    place = jnp.stack([core, zh, zq, y]).astype(jnp.int32)
    rows, _ = spectra.shape[2:]
    window = NOUT * rows // 512
    half = window // 2
    first = core == 0

    def ordered(block):
        return block.reshape((2, 2, 2, 2, 2) + block.shape[2:])

    passed = swap_core(lax.dynamic_slice_in_dim(spectra, (1 - core) * half, half, 2))
    a = ordered(jnp.where(first, spectra[:, :, :half], passed)).transpose(1, 3, 2, 4, 0, 5, 6)
    a = a.reshape((8, 2, 2) + a.shape[5:])
    b = jnp.where(first, jnp.concatenate([spectra[:, :, window:], passed], 2), spectra[:, :, half:])
    b = [ordered(b)[:, :, :, :, g].transpose(1, 3, 2, 0, 4, 5) for g in range(2)]
    b = [b[g].reshape((8, 2) + b[g].shape[4:]) for g in range(2)]
    b = lax.optimization_barrier(b)

    def exchange(block):
        return lax.all_to_all(block, ("x", "zr"), split_axis=0, concat_axis=0, tiled=True)

    a_own = exchange(a)
    a_own, *b = lax.optimization_barrier((a_own, *b))
    a_peer = swap_core(a_own)
    b_own, b_peer = [], []
    for g in range(2):
        b_own.append(exchange(b[g]))
        b_peer.append(swap_core(b_own[g]))

    shots = a_own.reshape((4, 2) + a_own.shape[1:])[:, 0]
    near, far = shots[:2], shots[2:]
    near, far = lax.optimization_barrier((near, far))
    across = send(near, lambda q, r, c, x, y, h: (0, r, c, x, y, 1 - h) if q == 0 else None)
    up = send(far, lambda q, r, c, x, y, h: (1, r, c, x, y, h) if q == 0 else None)
    down = send(far, lambda q, r, c, x, y, h: (1, r, c, x, y, 1 - h) if q == 0 else None)
    mine, others = jnp.where(zq == 0, near, up), jnp.where(zq == 0, across, down)
    pieces = [jnp.stack([mine[:, g], others[:, g]]) for g in range(2)]

    def turn(g):
        plus, minus, two = (
            lax.ppermute(pieces[g], "y", [(i, (i + s) % 4) for i in range(4)]) for s in (1, 3, 2)
        )
        return pieces[g], plus, two, minus

    turned = [turn(g) for g in range(2)]

    def homeward(blocks):
        return [
            send(
                block,
                lambda q, r, c, x, y, h: (x // 2, r, x % 2, (2 * q + c) ^ t, y, h),
            )
            for t, block in enumerate(blocks)
        ]

    def finish(g, blocks):
        pair = [blocks[0] + blocks[2], blocks[1] + blocks[3]]
        pair = [
            jnp.stack(
                [
                    -(wavelet[0, g] * p[0] - wavelet[1, g] * p[1]),
                    -(wavelet[0, g] * p[1] + wavelet[1, g] * p[0]),
                ]
            ).astype(jnp.bfloat16)
            for p in pair
        ]
        even = x % 2 == 0
        return jnp.concatenate(
            [jnp.where(even, pair[0], pair[1]), jnp.where(even, pair[1], pair[0])], 1
        )

    blocks = []
    for g in range(2):
        partial = contract(g, place, turned[g], a_own, a_peer, b_own[g], b_peer[g])
        blocks.append(homeward(partial))
    early = finish(0, blocks[0])
    late, early = lax.optimization_barrier((blocks[1], early))
    return jnp.stack([early, finish(1, late)], 1)


def solution(mesh):
    fine = Mesh(mesh.devices.reshape(SIZES), AXES)
    freq, col = AXES[:3], AXES[3:]
    return jax.shard_map(
        step,
        mesh=fine,
        in_specs=(P(None, None, freq, col), P(None, freq)),
        out_specs=P(None, freq, None, col),
        check_vma=False,
    )
```

```python
import jax
import jax.numpy as jnp
from jax import lax
from jax.experimental import pallas as pl
from jax.experimental.pallas import tpu as pltpu
from jax.sharding import Mesh, PartitionSpec as P


NOUT = 384
AXES = ("zq", "zr", "core", "x", "y", "zh")
SIZES = (2, 2, 2, 4, 4, 2)


def coordinates():
    out = [()]
    for size in SIZES:
        out = [c + (i,) for c in out for i in range(size)]
    return out


def flat(c):
    index = 0
    for i, size in zip(c, SIZES):
        index = index * size + i
    return index


def moved(target):
    pairs = []
    for c in coordinates():
        t = target(*c)
        if t is not None:
            pairs.append((flat(c), flat(t)))
    return pairs


def send(value, target):
    return lax.ppermute(value, AXES, moved(target))


def swap_core(value):
    return lax.ppermute(value, "core", [(0, 1), (1, 0)])


def contract(g, place, turned, a_own, a_peer, b_own, b_peer):
    half, lanes = turned[0].shape[-2:]
    depth = 16 * lanes

    def kernel(place_ref, u0, u1, u2, u3, ao_ref, ap_ref, bo_ref, bp_ref, o0, o1, o2, o3, left):
        core, zh, zq, y = place_ref[0], place_ref[1], place_ref[2], place_ref[3]
        for step, u_ref in enumerate((u0, u1, u2, u3)):
            ys = (y + 4 - step) % 4
            for xl in range(2):
                for piece in range(2):
                    start = pl.multiple_of(((xl * 4 + ys) * 2 + (piece ^ zh)) * lanes, lanes)
                    for part in range(2):
                        left[part * half : (part + 1) * half, pl.ds(start, lanes)] = u_ref[piece, xl, part]

        first = core == 0
        for t, out in enumerate((o0, o1, o2, o3)):
            x = (2 * zq + core) ^ t
            rows = []
            for zr in range(2):
                i = 2 * x + zr
                parts = []
                for part in range(2):
                    ao, ap = ao_ref[i, g, part], ap_ref[i, g, part]
                    bo, bp = bo_ref[i, part], bp_ref[i, part]
                    parts.append(
                        jnp.concatenate(
                            [
                                jnp.where(first, ao, ap),
                                jnp.where(first, ap, ao),
                                jnp.where(first, bo, bp),
                                jnp.where(first, bp, bo),
                            ],
                            0,
                        )
                    )
                rows.append(jnp.concatenate(parts, 1))
            right = jnp.concatenate(rows, 0)
            both = jnp.dot(left[...], right, preferred_element_type=jnp.float32)
            out[0] = both[:half, :lanes] - both[half:, lanes:]
            out[1] = both[:half, lanes:] + both[half:, :lanes]

    vmem = pl.BlockSpec(memory_space=pltpu.VMEM)
    result = jax.ShapeDtypeStruct((2, half, lanes), jnp.float32)
    return pl.pallas_call(
        kernel,
        out_shape=(result,) * 4,
        in_specs=[pl.BlockSpec(memory_space=pltpu.SMEM)] + [vmem] * 8,
        out_specs=(vmem,) * 4,
        scratch_shapes=[pltpu.VMEM((2 * half, depth), jnp.bfloat16)],
        cost_estimate=pl.CostEstimate(
            flops=2 * 2 * half * depth * 8 * lanes, bytes_accessed=7 << 20, transcendentals=0
        ),
        compiler_params=pltpu.CompilerParams(vmem_limit_bytes=40 << 20),
    )(place, *turned, a_own, a_peer, b_own, b_peer)


def step(spectra, wavelet):
    zq, core, x = lax.axis_index("zq"), lax.axis_index("core"), lax.axis_index("x")
    y, zh = lax.axis_index("y"), lax.axis_index("zh")
    place = jnp.stack([core, zh, zq, y]).astype(jnp.int32)
    rows, _ = spectra.shape[2:]
    window = NOUT * rows // 512
    half = window // 2
    first = core == 0

    def ordered(block):
        return block.reshape((2, 2, 4, 2) + block.shape[2:])

    passed = swap_core(lax.dynamic_slice_in_dim(spectra, (1 - core) * half, half, 2))
    a = ordered(jnp.where(first, spectra[:, :, :half], passed)).transpose(2, 1, 3, 0, 4, 5)
    a = a.reshape((8, 2, 2) + a.shape[4:])
    b = jnp.where(first, jnp.concatenate([spectra[:, :, window:], passed], 2), spectra[:, :, half:])
    b = [ordered(b)[:, :, :, g].transpose(2, 1, 0, 3, 4) for g in range(2)]
    b = [b[g].reshape((8, 2) + b[g].shape[3:]) for g in range(2)]
    b = lax.optimization_barrier(b)

    def exchange(block):
        return lax.all_to_all(block, ("x", "zr"), split_axis=0, concat_axis=0, tiled=True)

    a_own = exchange(a)
    a_own, *b = lax.optimization_barrier((a_own, *b))
    a_peer = swap_core(a_own)
    b_own, b_peer = [], []
    for g in range(2):
        b_own.append(exchange(b[g]))
        b_peer.append(swap_core(b_own[g]))

    def turn(g):
        shots = a_own.reshape((4, 2) + a_own.shape[1:])[:, 0, g]
        near, far = shots[:2], shots[2:]
        across = send(near, lambda q, r, c, x, y, h: (0, r, c, x, y, 1 - h) if q == 0 else None)
        up = send(far, lambda q, r, c, x, y, h: (1, r, c, x, y, h) if q == 0 else None)
        down = send(far, lambda q, r, c, x, y, h: (1, r, c, x, y, 1 - h) if q == 0 else None)
        mine, across, up, down = lax.optimization_barrier((near, across, up, down))
        pieces = jnp.stack([jnp.where(zq == 0, mine, up), jnp.where(zq == 0, across, down)])
        plus, minus, two = (
            lax.ppermute(pieces, "y", [(i, (i + s) % 4) for i in range(4)]) for s in (1, 3, 2)
        )
        return pieces, plus, two, minus

    turned = [turn(g) for g in range(2)]

    def homeward(blocks):
        return [
            send(
                block,
                lambda q, r, c, x, y, h: (r, x // 2, x % 2, (2 * q + c) ^ t, y, h),
            )
            for t, block in enumerate(blocks)
        ]

    def finish(g, blocks):
        pair = [blocks[0] + blocks[2], blocks[1] + blocks[3]]
        pair = [
            jnp.stack(
                [
                    -(wavelet[0, g] * p[0] - wavelet[1, g] * p[1]),
                    -(wavelet[0, g] * p[1] + wavelet[1, g] * p[0]),
                ]
            ).astype(jnp.bfloat16)
            for p in pair
        ]
        even = x % 2 == 0
        return jnp.concatenate(
            [jnp.where(even, pair[0], pair[1]), jnp.where(even, pair[1], pair[0])], 1
        )

    blocks = []
    for g in range(2):
        partial = contract(g, place, turned[g], a_own, a_peer, b_own[g], b_peer[g])
        blocks.append(homeward(partial))
    early = finish(0, blocks[0])
    late, early = lax.optimization_barrier((blocks[1], early))
    return jnp.stack([early, finish(1, late)], 1)


def solution(mesh):
    fine = Mesh(mesh.devices.reshape(SIZES), AXES)
    freq, col = AXES[:3], AXES[3:]
    return jax.shard_map(
        step,
        mesh=fine,
        in_specs=(P(None, None, freq, col), P(None, freq)),
        out_specs=P(None, freq, None, col),
        check_vma=False,
    )
```

```python
import jax
import jax.numpy as jnp
from jax import lax
from jax.experimental import pallas as pl
from jax.experimental.pallas import tpu as pltpu
from jax.sharding import Mesh, PartitionSpec as P


NOUT = 384
AXES = ("zq", "zr", "core", "x", "y", "zh")
SIZES = (2, 2, 2, 4, 4, 2)


def coordinates():
    out = [()]
    for size in SIZES:
        out = [c + (i,) for c in out for i in range(size)]
    return out


def flat(c):
    index = 0
    for i, size in zip(c, SIZES):
        index = index * size + i
    return index


def moved(target):
    pairs = []
    for c in coordinates():
        t = target(*c)
        if t is not None:
            pairs.append((flat(c), flat(t)))
    return pairs


def send(value, target):
    return lax.ppermute(value, AXES, moved(target))


def swap_core(value):
    return lax.ppermute(value, "core", [(0, 1), (1, 0)])


def contract(g, place, turned, a_own, a_peer, b_own, b_peer):
    half, lanes = turned[0].shape[-2:]
    depth = 16 * lanes

    def kernel(place_ref, u0, u1, u2, u3, ao_ref, ap_ref, bo_ref, bp_ref, o0, o1, o2, o3, left):
        core, zh, zq, y = place_ref[0], place_ref[1], place_ref[2], place_ref[3]
        for step, u_ref in enumerate((u0, u1, u2, u3)):
            ys = (y + 4 - step) % 4
            for xl in range(2):
                for piece in range(2):
                    start = pl.multiple_of(((xl * 4 + ys) * 2 + (piece ^ zh)) * lanes, lanes)
                    for part in range(2):
                        left[part * half : (part + 1) * half, pl.ds(start, lanes)] = u_ref[piece, xl, part]

        first = core == 0
        for t, out in enumerate((o0, o1, o2, o3)):
            x = (2 * zq + core) ^ t
            rows = []
            for zr in range(2):
                i = 2 * x + zr
                parts = []
                for part in range(2):
                    ao, ap = ao_ref[i, g, part], ap_ref[i, g, part]
                    bo, bp = bo_ref[i, part], bp_ref[i, part]
                    parts.append(
                        jnp.concatenate(
                            [
                                jnp.where(first, ao, ap),
                                jnp.where(first, ap, ao),
                                jnp.where(first, bo, bp),
                                jnp.where(first, bp, bo),
                            ],
                            0,
                        )
                    )
                rows.append(jnp.concatenate(parts, 1))
            right = jnp.concatenate(rows, 0)
            both = jnp.dot(left[...], right, preferred_element_type=jnp.float32)
            out[0] = both[:half, :lanes] - both[half:, lanes:]
            out[1] = both[:half, lanes:] + both[half:, :lanes]

    vmem = pl.BlockSpec(memory_space=pltpu.VMEM)
    result = jax.ShapeDtypeStruct((2, half, lanes), jnp.float32)
    return pl.pallas_call(
        kernel,
        out_shape=(result,) * 4,
        in_specs=[pl.BlockSpec(memory_space=pltpu.SMEM)] + [vmem] * 8,
        out_specs=(vmem,) * 4,
        scratch_shapes=[pltpu.VMEM((2 * half, depth), jnp.bfloat16)],
        cost_estimate=pl.CostEstimate(
            flops=2 * 2 * half * depth * 8 * lanes, bytes_accessed=7 << 20, transcendentals=0
        ),
        compiler_params=pltpu.CompilerParams(vmem_limit_bytes=40 << 20),
    )(place, *turned, a_own, a_peer, b_own, b_peer)


def finish(odd, wavelet, *blocks):
    half, lanes = blocks[0].shape[1:]

    def kernel(odd_ref, wave_ref, *refs):
        for g in range(2):
            wave_real, wave_imag = wave_ref[0, g], wave_ref[1, g]
            for t in range(2):
                start = pl.multiple_of((odd_ref[0] ^ t) * half, half)
                one, two = refs[4 * g + t], refs[4 * g + t + 2]
                real, imag = one[0] + two[0], one[1] + two[1]
                refs[8][0, g, pl.ds(start, half)] = (-(wave_real * real - wave_imag * imag)).astype(jnp.bfloat16)
                refs[8][1, g, pl.ds(start, half)] = (-(wave_real * imag + wave_imag * real)).astype(jnp.bfloat16)

    smem, vmem = pl.BlockSpec(memory_space=pltpu.SMEM), pl.BlockSpec(memory_space=pltpu.VMEM)
    return pl.pallas_call(
        kernel,
        out_shape=jax.ShapeDtypeStruct((2, 2, 2 * half, lanes), jnp.bfloat16),
        in_specs=[smem, smem] + [vmem] * 8,
        out_specs=vmem,
        cost_estimate=pl.CostEstimate(flops=8 * 4 * half * lanes, bytes_accessed=2 << 20, transcendentals=0),
    )(odd, wavelet, *blocks)


def step(spectra, wavelet):
    zq, core, x = lax.axis_index("zq"), lax.axis_index("core"), lax.axis_index("x")
    y, zh = lax.axis_index("y"), lax.axis_index("zh")
    place = jnp.stack([core, zh, zq, y]).astype(jnp.int32)
    rows, _ = spectra.shape[2:]
    window = NOUT * rows // 512
    half = window // 2
    first = core == 0

    def ordered(block):
        return block.reshape((2, 2, 4, 2) + block.shape[2:])

    passed = swap_core(lax.dynamic_slice_in_dim(spectra, (1 - core) * half, half, 2))
    a = ordered(jnp.where(first, spectra[:, :, :half], passed)).transpose(2, 1, 3, 0, 4, 5)
    a = a.reshape((8, 2, 2) + a.shape[4:])
    b = jnp.where(first, jnp.concatenate([spectra[:, :, window:], passed], 2), spectra[:, :, half:])
    b = [ordered(b)[:, :, :, g].transpose(2, 1, 0, 3, 4) for g in range(2)]
    b = [b[g].reshape((8, 2) + b[g].shape[3:]) for g in range(2)]
    b = lax.optimization_barrier(b)

    def exchange(block):
        return lax.all_to_all(block, ("x", "zr"), split_axis=0, concat_axis=0, tiled=True)

    a_own = exchange(a)
    a_own, *b = lax.optimization_barrier((a_own, *b))
    a_peer = swap_core(a_own)
    b_own, b_peer = [], []
    for g in range(2):
        b_own.append(exchange(b[g]))
        b_peer.append(swap_core(b_own[g]))

    def turn(g):
        shots = a_own.reshape((4, 2) + a_own.shape[1:])[:, 0, g]
        near, far = shots[:2], shots[2:]
        across = send(near, lambda q, r, c, x, y, h: (0, r, c, x, y, 1 - h) if q == 0 else None)
        up = send(far, lambda q, r, c, x, y, h: (1, r, c, x, y, h) if q == 0 else None)
        down = send(far, lambda q, r, c, x, y, h: (1, r, c, x, y, 1 - h) if q == 0 else None)
        mine, across, up, down = lax.optimization_barrier((near, across, up, down))
        pieces = jnp.stack([jnp.where(zq == 0, mine, up), jnp.where(zq == 0, across, down)])
        plus, minus, two = (
            lax.ppermute(pieces, "y", [(i, (i + s) % 4) for i in range(4)]) for s in (1, 3, 2)
        )
        return pieces, plus, two, minus

    turned = [turn(g) for g in range(2)]

    def homeward(blocks):
        return [
            send(
                block,
                lambda q, r, c, x, y, h: (r, x // 2, x % 2, (2 * q + c) ^ t, y, h),
            )
            for t, block in enumerate(blocks)
        ]

    blocks = []
    for g in range(2):
        partial = contract(g, place, turned[g], a_own, a_peer, b_own[g], b_peer[g])
        blocks.append(homeward(partial))
    return finish(jnp.stack([x % 2]).astype(jnp.int32), wavelet, *blocks[0], *blocks[1])


def solution(mesh):
    fine = Mesh(mesh.devices.reshape(SIZES), AXES)
    freq, col = AXES[:3], AXES[3:]
    return jax.shard_map(
        step,
        mesh=fine,
        in_specs=(P(None, None, freq, col), P(None, freq)),
        out_specs=P(None, freq, None, col),
        check_vma=False,
    )
```

```python
import jax
import jax.numpy as jnp
from jax import lax
from jax.experimental import pallas as pl
from jax.experimental.pallas import tpu as pltpu
from jax.sharding import Mesh, PartitionSpec as P


NOUT = 384
AXES = ("zq", "zr", "core", "x", "y", "zh")
SIZES = (2, 2, 2, 4, 4, 2)


def coordinates():
    out = [()]
    for size in SIZES:
        out = [c + (i,) for c in out for i in range(size)]
    return out


def flat(c):
    index = 0
    for i, size in zip(c, SIZES):
        index = index * size + i
    return index


def moved(target):
    pairs = []
    for c in coordinates():
        t = target(*c)
        if t is not None:
            pairs.append((flat(c), flat(t)))
    return pairs


def send(value, target):
    return lax.ppermute(value, AXES, moved(target))


def swap_core(value):
    return lax.ppermute(value, "core", [(0, 1), (1, 0)])


def contract(g, place, turned, a_own, a_peer, b_own, b_peer, near=False, far=()):
    half, lanes = turned[0].shape[-2:]
    depth = 16 * lanes
    given = (a_own, a_peer, b_own, b_peer)
    operands = given if not (near or far) else (given[:3] if near else (b_peer, *far))

    def kernel(place_ref, u0, u1, u2, u3, *refs):
        refs, outs, left = refs[: len(operands)], refs[len(operands) : -1], refs[-1]
        core, zh, zq, y = place_ref[0], place_ref[1], place_ref[2], place_ref[3]
        for step, u_ref in enumerate((u0, u1, u2, u3)):
            ys = (y + 4 - step) % 4
            for xl in range(2):
                for piece in range(2):
                    start = pl.multiple_of(((xl * 4 + ys) * 2 + (piece ^ zh)) * lanes, lanes)
                    for part in range(2):
                        left[part * half : (part + 1) * half, pl.ds(start, lanes)] = u_ref[piece, xl, part]

        first = core == 0
        gap = 3 * lanes - (8 * lanes - 2 * half) // 2
        blank = jnp.zeros((gap, lanes), jnp.bfloat16)

        def window(ref, i, part, early):
            value = ref[i, part]
            return jnp.where(early, jnp.concatenate([value, blank], 0), jnp.concatenate([blank, value], 0))

        for t, out in enumerate(outs):
            x = (2 * zq + core) ^ t
            both = None
            for zr in range(2):
                i = 2 * x + zr
                base = 8 * zr * lanes
                columns = []
                if not far:
                    ao_ref, ap_ref, bo_ref = refs[:3]
                    top = []
                    for part in range(2):
                        ao, ap = ao_ref[i, g, part], ap_ref[i, g, part]
                        top.append([jnp.where(first, ao, ap), jnp.where(first, ap, ao)])
                if not (near or far):
                    bp_ref = refs[3]
                    for part in range(2):
                        bo, bp = bo_ref[i, part], bp_ref[i, part]
                        top[part] += [jnp.where(first, bo, bp), jnp.where(first, bp, bo)]
                    columns.append((left[:, base : base + 8 * lanes], top))
                elif near:
                    columns.append((left[:, base : base + 3 * lanes], top))
                if near or far:
                    early = first if near else jnp.logical_not(first)
                    start = pl.multiple_of(base + jnp.where(early, 3, 5) * lanes, lanes)
                    ref = refs[2] if near else refs[0]
                    rows = [[window(ref, i, part, early)] for part in range(2)]
                    columns.append((left[:, pl.ds(start, 3 * lanes)], rows))
                for lhs, rows in columns:
                    rhs = jnp.concatenate([jnp.concatenate(r, 0) for r in rows], 1)
                    term = jnp.dot(lhs, rhs, preferred_element_type=jnp.float32)
                    both = term if both is None else both + term
            real = both[:half, :lanes] - both[half:, lanes:]
            imag = both[:half, lanes:] + both[half:, :lanes]
            if far:
                real, imag = refs[1 + t][0] + real, refs[1 + t][1] + imag
            out[0] = real
            out[1] = imag

    vmem = pl.BlockSpec(memory_space=pltpu.VMEM)
    result = jax.ShapeDtypeStruct((2, half, lanes), jnp.float32)
    return pl.pallas_call(
        kernel,
        out_shape=(result,) * 4,
        in_specs=[pl.BlockSpec(memory_space=pltpu.SMEM)] + [vmem] * (4 + len(operands)),
        out_specs=(vmem,) * 4,
        scratch_shapes=[pltpu.VMEM((2 * half, depth), jnp.bfloat16)],
        cost_estimate=pl.CostEstimate(
            flops=2 * 2 * half * depth * 8 * lanes, bytes_accessed=7 << 20, transcendentals=0
        ),
        compiler_params=pltpu.CompilerParams(vmem_limit_bytes=40 << 20),
    )(place, *turned, *operands)


def finish(odd, wavelet, *blocks):
    half, lanes = blocks[0].shape[1:]

    def kernel(odd_ref, wave_ref, *refs):
        for g in range(2):
            wave_real, wave_imag = wave_ref[0, g], wave_ref[1, g]
            for t in range(2):
                start = pl.multiple_of((odd_ref[0] ^ t) * half, half)
                one, two = refs[4 * g + t], refs[4 * g + t + 2]
                real, imag = one[0] + two[0], one[1] + two[1]
                refs[8][0, g, pl.ds(start, half)] = (-(wave_real * real - wave_imag * imag)).astype(jnp.bfloat16)
                refs[8][1, g, pl.ds(start, half)] = (-(wave_real * imag + wave_imag * real)).astype(jnp.bfloat16)

    smem, vmem = pl.BlockSpec(memory_space=pltpu.SMEM), pl.BlockSpec(memory_space=pltpu.VMEM)
    return pl.pallas_call(
        kernel,
        out_shape=jax.ShapeDtypeStruct((2, 2, 2 * half, lanes), jnp.bfloat16),
        in_specs=[smem, smem] + [vmem] * 8,
        out_specs=vmem,
        cost_estimate=pl.CostEstimate(flops=8 * 4 * half * lanes, bytes_accessed=2 << 20, transcendentals=0),
    )(odd, wavelet, *blocks)


def step(spectra, wavelet):
    zq, core, x = lax.axis_index("zq"), lax.axis_index("core"), lax.axis_index("x")
    y, zh = lax.axis_index("y"), lax.axis_index("zh")
    place = jnp.stack([core, zh, zq, y]).astype(jnp.int32)
    rows, _ = spectra.shape[2:]
    window = NOUT * rows // 512
    half = window // 2
    first = core == 0

    def ordered(block):
        return block.reshape((2, 2, 4, 2) + block.shape[2:])

    passed = swap_core(lax.dynamic_slice_in_dim(spectra, (1 - core) * half, half, 2))
    a = ordered(jnp.where(first, spectra[:, :, :half], passed)).transpose(2, 1, 3, 0, 4, 5)
    a = a.reshape((8, 2, 2) + a.shape[4:])
    b = jnp.where(first, jnp.concatenate([spectra[:, :, window:], passed], 2), spectra[:, :, half:])
    b = [ordered(b)[:, :, :, g].transpose(2, 1, 0, 3, 4) for g in range(2)]
    b = [b[g].reshape((8, 2) + b[g].shape[3:]) for g in range(2)]
    b = lax.optimization_barrier(b)

    def exchange(block):
        return lax.all_to_all(block, ("x", "zr"), split_axis=0, concat_axis=0, tiled=True)

    a_own = exchange(a)
    a_own, *b = lax.optimization_barrier((a_own, *b))
    a_peer = swap_core(a_own)
    b_own, b_peer = [], []
    for g in range(2):
        b_own.append(exchange(b[g]))
        b_peer.append(swap_core(b_own[g]))

    def turn(g):
        shots = a_own.reshape((4, 2) + a_own.shape[1:])[:, 0, g]
        near, far = shots[:2], shots[2:]
        across = send(near, lambda q, r, c, x, y, h: (0, r, c, x, y, 1 - h) if q == 0 else None)
        up = send(far, lambda q, r, c, x, y, h: (1, r, c, x, y, h) if q == 0 else None)
        down = send(far, lambda q, r, c, x, y, h: (1, r, c, x, y, 1 - h) if q == 0 else None)
        mine, across, up, down = lax.optimization_barrier((near, across, up, down))
        pieces = jnp.stack([jnp.where(zq == 0, mine, up), jnp.where(zq == 0, across, down)])
        plus, minus, two = (
            lax.ppermute(pieces, "y", [(i, (i + s) % 4) for i in range(4)]) for s in (1, 3, 2)
        )
        return pieces, plus, two, minus

    turned = [turn(g) for g in range(2)]

    def homeward(blocks):
        return [
            send(
                block,
                lambda q, r, c, x, y, h: (r, x // 2, x % 2, (2 * q + c) ^ t, y, h),
            )
            for t, block in enumerate(blocks)
        ]

    partial = contract(0, place, turned[0], a_own, a_peer, b_own[0], b_peer[0])
    blocks = [homeward(partial)]
    partial = contract(1, place, turned[1], a_own, a_peer, b_own[1], None, near=True)
    partial = contract(1, place, turned[1], None, None, None, b_peer[1], far=partial)
    blocks.append(homeward(partial))
    return finish(jnp.stack([x % 2]).astype(jnp.int32), wavelet, *blocks[0], *blocks[1])


def solution(mesh):
    fine = Mesh(mesh.devices.reshape(SIZES), AXES)
    freq, col = AXES[:3], AXES[3:]
    return jax.shard_map(
        step,
        mesh=fine,
        in_specs=(P(None, None, freq, col), P(None, freq)),
        out_specs=P(None, freq, None, col),
        check_vma=False,
    )
```

```python
import jax
import jax.numpy as jnp
from jax import lax
from jax.experimental import pallas as pl
from jax.experimental.pallas import tpu as pltpu
from jax.sharding import Mesh, PartitionSpec as P


NOUT = 384
AXES = ("zq", "zr", "core", "x", "y", "zh")
SIZES = (2, 2, 2, 4, 4, 2)


def coordinates():
    out = [()]
    for size in SIZES:
        out = [c + (i,) for c in out for i in range(size)]
    return out


def flat(c):
    index = 0
    for i, size in zip(c, SIZES):
        index = index * size + i
    return index


def moved(target):
    pairs = []
    for c in coordinates():
        t = target(*c)
        if t is not None:
            pairs.append((flat(c), flat(t)))
    return pairs


def send(value, target):
    return lax.ppermute(value, AXES, moved(target))


def swap_core(value):
    return lax.ppermute(value, "core", [(0, 1), (1, 0)])


def contract(g, k, place, turned, a_own, a_peer, b_own, b_peer):
    half, lanes = turned[0].shape[-2:]
    depth = 16 * lanes

    def kernel(place_ref, u0, u1, u2, u3, ao_ref, ap_ref, bo_ref, bp_ref, o0, o1, left):
        core, zh, zq, y = place_ref[0], place_ref[1], place_ref[2], place_ref[3]
        for step, u_ref in enumerate((u0, u1, u2, u3)):
            ys = (y + 4 - step) % 4
            for xl in range(2):
                for piece in range(2):
                    start = pl.multiple_of(((xl * 4 + ys) * 2 + (piece ^ zh)) * lanes, lanes)
                    for part in range(2):
                        left[part * half : (part + 1) * half, pl.ds(start, lanes)] = u_ref[piece, xl, part]

        first = core == 0
        for t, out in ((k, o0), (k + 2, o1)):
            x = (2 * zq + core) ^ t
            rows = []
            for zr in range(2):
                i = 2 * x + zr
                parts = []
                for part in range(2):
                    ao, ap = ao_ref[i, g, part], ap_ref[i, g, part]
                    bo, bp = bo_ref[i, part], bp_ref[i, part]
                    parts.append(
                        jnp.concatenate(
                            [
                                jnp.where(first, ao, ap),
                                jnp.where(first, ap, ao),
                                jnp.where(first, bo, bp),
                                jnp.where(first, bp, bo),
                            ],
                            0,
                        )
                    )
                rows.append(jnp.concatenate(parts, 1))
            right = jnp.concatenate(rows, 0)
            both = jnp.dot(left[...], right, preferred_element_type=jnp.float32)
            out[0] = both[:half, :lanes] - both[half:, lanes:]
            out[1] = both[:half, lanes:] + both[half:, :lanes]

    vmem = pl.BlockSpec(memory_space=pltpu.VMEM)
    result = jax.ShapeDtypeStruct((2, half, lanes), jnp.float32)
    return pl.pallas_call(
        kernel,
        out_shape=(result,) * 2,
        in_specs=[pl.BlockSpec(memory_space=pltpu.SMEM)] + [vmem] * 8,
        out_specs=(vmem,) * 2,
        scratch_shapes=[pltpu.VMEM((2 * half, depth), jnp.bfloat16)],
        cost_estimate=pl.CostEstimate(
            flops=2 * 2 * half * depth * 4 * lanes, bytes_accessed=7 << 20, transcendentals=0
        ),
        compiler_params=pltpu.CompilerParams(vmem_limit_bytes=40 << 20),
    )(place, *turned, a_own, a_peer, b_own, b_peer)


def finish(g, k, odd, wavelet, blocks, prior=()):
    half, lanes = blocks[0].shape[1:]

    def kernel(odd_ref, wave_ref, one, two, *refs):
        wave_real, wave_imag = wave_ref[0, g], wave_ref[1, g]
        out = refs[-1]
        real, imag = one[0] + two[0], one[1] + two[1]
        out[0, 0] = (-(wave_real * real - wave_imag * imag)).astype(jnp.bfloat16)
        out[1, 0] = (-(wave_real * imag + wave_imag * real)).astype(jnp.bfloat16)

    whole = pl.BlockSpec((2, half, lanes), lambda i, odd_ref: (0, 0, 0))
    return pl.pallas_call(
        kernel,
        grid_spec=pltpu.PrefetchScalarGridSpec(
            num_scalar_prefetch=1,
            grid=(1,),
            in_specs=[pl.BlockSpec(memory_space=pltpu.SMEM), whole, whole]
            + [pl.BlockSpec(memory_space=pl.ANY)] * len(prior),
            out_specs=pl.BlockSpec((2, 1, half, lanes), lambda i, odd_ref: (0, g, odd_ref[0] ^ k, 0)),
        ),
        out_shape=jax.ShapeDtypeStruct((2, 2, 2 * half, lanes), jnp.bfloat16),
        input_output_aliases={4: 0} if prior else {},
        cost_estimate=pl.CostEstimate(flops=8 * half * lanes, bytes_accessed=1 << 20, transcendentals=0),
    )(odd, wavelet, *blocks, *prior)


def step(spectra, wavelet):
    zq, core, x = lax.axis_index("zq"), lax.axis_index("core"), lax.axis_index("x")
    y, zh = lax.axis_index("y"), lax.axis_index("zh")
    place = jnp.stack([core, zh, zq, y]).astype(jnp.int32)
    rows, _ = spectra.shape[2:]
    window = NOUT * rows // 512
    half = window // 2
    first = core == 0

    def ordered(block):
        return block.reshape((2, 2, 4, 2) + block.shape[2:])

    passed = swap_core(lax.dynamic_slice_in_dim(spectra, (1 - core) * half, half, 2))
    a = ordered(jnp.where(first, spectra[:, :, :half], passed)).transpose(2, 1, 3, 0, 4, 5)
    a = a.reshape((8, 2, 2) + a.shape[4:])
    b = jnp.where(first, jnp.concatenate([spectra[:, :, window:], passed], 2), spectra[:, :, half:])
    b = [ordered(b)[:, :, :, g].transpose(2, 1, 0, 3, 4) for g in range(2)]
    b = [b[g].reshape((8, 2) + b[g].shape[3:]) for g in range(2)]
    b = lax.optimization_barrier(b)

    def exchange(block):
        return lax.all_to_all(block, ("x", "zr"), split_axis=0, concat_axis=0, tiled=True)

    a_own = exchange(a)
    a_own, *b = lax.optimization_barrier((a_own, *b))
    a_peer = swap_core(a_own)
    b_own, b_peer = [], []
    for g in range(2):
        b_own.append(exchange(b[g]))
        b_peer.append(swap_core(b_own[g]))

    def turn(g):
        shots = a_own.reshape((4, 2) + a_own.shape[1:])[:, 0, g]
        near, far = shots[:2], shots[2:]
        across = send(near, lambda q, r, c, x, y, h: (0, r, c, x, y, 1 - h) if q == 0 else None)
        up = send(far, lambda q, r, c, x, y, h: (1, r, c, x, y, h) if q == 0 else None)
        down = send(far, lambda q, r, c, x, y, h: (1, r, c, x, y, 1 - h) if q == 0 else None)
        mine, across, up, down = lax.optimization_barrier((near, across, up, down))
        pieces = jnp.stack([jnp.where(zq == 0, mine, up), jnp.where(zq == 0, across, down)])
        plus, minus, two = (
            lax.ppermute(pieces, "y", [(i, (i + s) % 4) for i in range(4)]) for s in (1, 3, 2)
        )
        return pieces, plus, two, minus

    turned = [turn(g) for g in range(2)]

    def homeward(k, blocks):
        return [
            send(block, lambda q, r, c, x, y, h: (r, x // 2, x % 2, (2 * q + c) ^ t, y, h))
            for t, block in zip((k, k + 2), blocks)
        ]

    arrived = []
    for g in range(2):
        for k in range(2):
            partial = contract(g, k, place, turned[g], a_own, a_peer, b_own[g], b_peer[g])
            arrived.append((g, k, homeward(k, partial)))
    odd = jnp.stack([x % 2]).astype(jnp.int32)
    result = ()
    for g, k, blocks in arrived:
        result = (finish(g, k, odd, wavelet, blocks, result),)
    return result[0]


def solution(mesh):
    fine = Mesh(mesh.devices.reshape(SIZES), AXES)
    freq, col = AXES[:3], AXES[3:]
    return jax.shard_map(
        step,
        mesh=fine,
        in_specs=(P(None, None, freq, col), P(None, freq)),
        out_specs=P(None, freq, None, col),
        check_vma=False,
    )
```

```python
import jax
import jax.numpy as jnp
from jax import lax
from jax.experimental import pallas as pl
from jax.experimental.pallas import tpu as pltpu
from jax.sharding import Mesh, PartitionSpec as P


NOUT = 384
AXES = ("zq", "zr", "core", "x", "y", "zh")
SIZES = (2, 2, 2, 4, 4, 2)


def coordinates():
    out = [()]
    for size in SIZES:
        out = [c + (i,) for c in out for i in range(size)]
    return out


def flat(c):
    index = 0
    for i, size in zip(c, SIZES):
        index = index * size + i
    return index


def moved(target):
    pairs = []
    for c in coordinates():
        t = target(*c)
        if t is not None:
            pairs.append((flat(c), flat(t)))
    return pairs


def send(value, target):
    return lax.ppermute(value, AXES, moved(target))


def swap_core(value):
    return lax.ppermute(value, "core", [(0, 1), (1, 0)])


def contract(g, place, turned, a_own, a_peer, b_own, b_peer):
    half, lanes = turned[0].shape[-2:]
    depth = 16 * lanes

    def kernel(place_ref, u0, u1, u2, u3, ao_ref, ap_ref, bo_ref, bp_ref, o0, o1, o2, o3, left):
        core, zh, y = place_ref[0], place_ref[1], place_ref[3]
        t = pl.program_id(0)

        @pl.when(t == 0)
        def _():
            for step, u_ref in enumerate((u0, u1, u2, u3)):
                ys = (y + 4 - step) % 4
                for xl in range(2):
                    for piece in range(2):
                        start = pl.multiple_of(((xl * 4 + ys) * 2 + (piece ^ zh)) * lanes, lanes)
                        for part in range(2):
                            left[part * half : (part + 1) * half, pl.ds(start, lanes)] = u_ref[piece, xl, part]

        first = core == 0
        rows = []
        for zr in range(2):
            parts = []
            for part in range(2):
                ao, ap = ao_ref[zr, 0, part], ap_ref[zr, 0, part]
                bo, bp = bo_ref[zr, part], bp_ref[zr, part]
                parts.append(
                    jnp.concatenate(
                        [
                            jnp.where(first, ao, ap),
                            jnp.where(first, ap, ao),
                            jnp.where(first, bo, bp),
                            jnp.where(first, bp, bo),
                        ],
                        0,
                    )
                )
            rows.append(jnp.concatenate(parts, 1))
        right = jnp.concatenate(rows, 0)
        both = jnp.dot(left[...], right, preferred_element_type=jnp.float32)
        real = both[:half, :lanes] - both[half:, lanes:]
        imag = both[:half, lanes:] + both[half:, :lanes]
        for i, out in enumerate((o0, o1, o2, o3)):

            @pl.when(t == i)
            def _():
                out[0] = real
                out[1] = imag

    def column(t, place_ref):
        return (2 * place_ref[2] + place_ref[0]) ^ t

    a_spec = pl.BlockSpec((2, 1, 2, half, lanes), lambda t, p: (column(t, p), g, 0, 0, 0))
    b_spec = pl.BlockSpec((2,) + b_own.shape[1:], lambda t, p: (column(t, p), 0, 0, 0))
    u_spec = pl.BlockSpec(turned[0].shape, lambda t, p: (0, 0, 0, 0, 0))
    result = jax.ShapeDtypeStruct((2, half, lanes), jnp.float32)
    return pl.pallas_call(
        kernel,
        out_shape=(result,) * 4,
        grid_spec=pltpu.PrefetchScalarGridSpec(
            num_scalar_prefetch=1,
            grid=(4,),
            in_specs=[u_spec] * 4 + [a_spec, a_spec, b_spec, b_spec],
            out_specs=(pl.BlockSpec((2, half, lanes), lambda t, p: (0, 0, 0)),) * 4,
            scratch_shapes=[pltpu.VMEM((2 * half, depth), jnp.bfloat16)],
        ),
        cost_estimate=pl.CostEstimate(
            flops=2 * 2 * half * depth * 8 * lanes, bytes_accessed=7 << 20, transcendentals=0
        ),
        compiler_params=pltpu.CompilerParams(vmem_limit_bytes=40 << 20),
    )(place, *turned, a_own, a_peer, b_own, b_peer)


def arrange(core, spectra, passed):
    half, lanes = passed.shape[2:]

    def kernel(core_ref, low_ref, passed_ref, out_ref):
        first = core_ref[0] == 0
        pair = 8 * pl.program_id(1) + 2 * pl.program_id(0)
        for g in range(2):
            for part in range(2):
                out_ref[0, g, part] = jnp.where(first, low_ref[part, g], passed_ref[part, pair + g])

    spec = pl.BlockSpec((2, 2, half, lanes), lambda x, zr, c: (0, 4 * zr + x, 0, 0))
    return pl.pallas_call(
        kernel,
        out_shape=jax.ShapeDtypeStruct((8, 2, 2, half, lanes), jnp.bfloat16),
        grid_spec=pltpu.PrefetchScalarGridSpec(
            num_scalar_prefetch=1,
            grid=(4, 2),
            in_specs=[spec, pl.BlockSpec(memory_space=pltpu.VMEM)],
            out_specs=pl.BlockSpec((1, 2, 2, half, lanes), lambda x, zr, c: (2 * x + zr, 0, 0, 0, 0)),
        ),
        cost_estimate=pl.CostEstimate(flops=0, bytes_accessed=5 << 20, transcendentals=0),
    )(core, spectra, passed)


def finish(g, odd, wavelet, blocks, prior=()):
    half, lanes = blocks[0].shape[1:]

    def kernel(odd_ref, wave_ref, *refs):
        wave_real, wave_imag = wave_ref[0, g], wave_ref[1, g]
        out = refs[-1]
        for t in range(2):
            start = pl.multiple_of((odd_ref[0] ^ t) * half, half)
            one, two = refs[t], refs[t + 2]
            real, imag = one[0] + two[0], one[1] + two[1]
            out[0, 0, pl.ds(start, half)] = (-(wave_real * real - wave_imag * imag)).astype(jnp.bfloat16)
            out[1, 0, pl.ds(start, half)] = (-(wave_real * imag + wave_imag * real)).astype(jnp.bfloat16)

    smem, vmem = pl.BlockSpec(memory_space=pltpu.SMEM), pl.BlockSpec(memory_space=pltpu.VMEM)
    return pl.pallas_call(
        kernel,
        grid=(1,),
        out_shape=jax.ShapeDtypeStruct((2, 2, 2 * half, lanes), jnp.bfloat16),
        in_specs=[smem, smem] + [vmem] * 4 + [pl.BlockSpec(memory_space=pl.ANY)] * len(prior),
        out_specs=pl.BlockSpec((2, 1, 2 * half, lanes), lambda i: (0, g, 0, 0)),
        input_output_aliases={6: 0} if prior else {},
        cost_estimate=pl.CostEstimate(flops=8 * 2 * half * lanes, bytes_accessed=1 << 20, transcendentals=0),
    )(odd, wavelet, *blocks, *prior)


def step(spectra, wavelet):
    zq, core, x = lax.axis_index("zq"), lax.axis_index("core"), lax.axis_index("x")
    y, zh = lax.axis_index("y"), lax.axis_index("zh")
    place = jnp.stack([core, zh, zq, y]).astype(jnp.int32)
    rows, _ = spectra.shape[2:]
    window = NOUT * rows // 512
    half = window // 2
    first = core == 0

    def ordered(block):
        return block.reshape((2, 2, 4, 2) + block.shape[2:])

    passed = swap_core(lax.dynamic_slice_in_dim(spectra, (1 - core) * half, half, 2))
    a = arrange(place, spectra, passed)
    b = jnp.where(first, jnp.concatenate([spectra[:, :, window:], passed], 2), spectra[:, :, half:])
    b = [ordered(b)[:, :, :, g].transpose(2, 1, 0, 3, 4) for g in range(2)]
    b = [b[g].reshape((8, 2) + b[g].shape[3:]) for g in range(2)]
    b = lax.optimization_barrier(b)

    def exchange(block):
        return lax.all_to_all(block, ("x", "zr"), split_axis=0, concat_axis=0, tiled=True)

    a_own = exchange(a)
    a_own, *b = lax.optimization_barrier((a_own, *b))
    a_peer = swap_core(a_own)
    b_own, b_peer = [], []
    for g in range(2):
        b_own.append(exchange(b[g]))
        b_peer.append(swap_core(b_own[g]))

    def turn(g):
        shots = a_own.reshape((4, 2) + a_own.shape[1:])[:, 0, g]
        near, far = shots[:2], shots[2:]
        across = send(near, lambda q, r, c, x, y, h: (0, r, c, x, y, 1 - h) if q == 0 else None)
        up = send(far, lambda q, r, c, x, y, h: (1, r, c, x, y, h) if q == 0 else None)
        down = send(far, lambda q, r, c, x, y, h: (1, r, c, x, y, 1 - h) if q == 0 else None)
        mine, across, up, down = lax.optimization_barrier((near, across, up, down))
        pieces = jnp.stack([jnp.where(zq == 0, mine, up), jnp.where(zq == 0, across, down)])
        plus, minus, two = (
            lax.ppermute(pieces, "y", [(i, (i + s) % 4) for i in range(4)]) for s in (1, 3, 2)
        )
        return pieces, plus, two, minus

    turned = [turn(g) for g in range(2)]

    def homeward(blocks):
        return [
            send(
                block,
                lambda q, r, c, x, y, h: (r, x // 2, x % 2, (2 * q + c) ^ t, y, h),
            )
            for t, block in enumerate(blocks)
        ]

    blocks = []
    for g in range(2):
        partial = contract(g, place, turned[g], a_own, a_peer, b_own[g], b_peer[g])
        blocks.append(homeward(partial))
    odd = jnp.stack([x % 2]).astype(jnp.int32)
    early = finish(0, odd, wavelet, blocks[0])
    return finish(1, odd, wavelet, blocks[1], (early,))


def solution(mesh):
    fine = Mesh(mesh.devices.reshape(SIZES), AXES)
    freq, col = AXES[:3], AXES[3:]
    return jax.shard_map(
        step,
        mesh=fine,
        in_specs=(P(None, None, freq, col), P(None, freq)),
        out_specs=P(None, freq, None, col),
        check_vma=False,
    )
```

```python
import jax
import jax.numpy as jnp
from jax import lax
from jax.experimental import pallas as pl
from jax.experimental.pallas import tpu as pltpu
from jax.sharding import Mesh, PartitionSpec as P


NOUT = 384
AXES = ("zq", "zr", "core", "x", "y", "zh")
SIZES = (2, 2, 2, 4, 4, 2)


def coordinates():
    out = [()]
    for size in SIZES:
        out = [c + (i,) for c in out for i in range(size)]
    return out


def flat(c):
    index = 0
    for i, size in zip(c, SIZES):
        index = index * size + i
    return index


def moved(target):
    pairs = []
    for c in coordinates():
        t = target(*c)
        if t is not None:
            pairs.append((flat(c), flat(t)))
    return pairs


def send(value, target):
    return lax.ppermute(value, AXES, moved(target))


def swap_core(value):
    return lax.ppermute(value, "core", [(0, 1), (1, 0)])


def contract(g, place, turned, a_own, a_peer, b_own, b_peer):
    half, lanes = turned[0].shape[-2:]
    depth = 16 * lanes

    def kernel(place_ref, u0, u1, u2, u3, ao_ref, ap_ref, bo_ref, bp_ref, o0, o1, o2, o3, left):
        core, zh, zq, y = place_ref[0], place_ref[1], place_ref[2], place_ref[3]
        for step, u_ref in enumerate((u0, u1, u2, u3)):
            ys = (y + 4 - step) % 4
            for xl in range(2):
                for piece in range(2):
                    start = pl.multiple_of(((xl * 4 + ys) * 2 + (piece ^ zh)) * lanes, lanes)
                    for part in range(2):
                        left[part * half : (part + 1) * half, pl.ds(start, lanes)] = u_ref[piece, xl, part]

        first = core == 0
        for t, out in enumerate((o0, o1, o2, o3)):
            x = (2 * zq + core) ^ t
            rows = []
            for zr in range(2):
                i = 2 * x + zr
                parts = []
                for part in range(2):
                    ao, ap = ao_ref[i, g, part], ap_ref[i, g, part]
                    bo, bp = bo_ref[i, part], bp_ref[i, part]
                    parts.append(
                        jnp.concatenate(
                            [
                                jnp.where(first, ao, ap),
                                jnp.where(first, ap, ao),
                                jnp.where(first, bo, bp),
                                jnp.where(first, bp, bo),
                            ],
                            0,
                        )
                    )
                rows.append(jnp.concatenate(parts, 1))
            right = jnp.concatenate(rows, 0)
            both = jnp.dot(left[...], right, preferred_element_type=jnp.float32)
            out[0] = both[:half, :lanes] - both[half:, lanes:]
            out[1] = both[:half, lanes:] + both[half:, :lanes]

    vmem = pl.BlockSpec(memory_space=pltpu.VMEM)
    result = jax.ShapeDtypeStruct((2, half, lanes), jnp.float32)
    return pl.pallas_call(
        kernel,
        out_shape=(result,) * 4,
        in_specs=[pl.BlockSpec(memory_space=pltpu.SMEM)] + [vmem] * 8,
        out_specs=(vmem,) * 4,
        scratch_shapes=[pltpu.VMEM((2 * half, depth), jnp.bfloat16)],
        cost_estimate=pl.CostEstimate(
            flops=2 * 2 * half * depth * 8 * lanes, bytes_accessed=7 << 20, transcendentals=0
        ),
        compiler_params=pltpu.CompilerParams(vmem_limit_bytes=40 << 20),
    )(place, *turned, a_own, a_peer, b_own, b_peer)


def finish(g, odd, wavelet, blocks, prior=()):
    half, lanes = blocks[0].shape[1:]

    def kernel(odd_ref, wave_ref, *refs):
        wave_real, wave_imag = wave_ref[0, g], wave_ref[1, g]
        out = refs[-1]
        for t in range(2):
            start = pl.multiple_of((odd_ref[0] ^ t) * half, half)
            one, two = refs[t], refs[t + 2]
            real, imag = one[0] + two[0], one[1] + two[1]
            out[0, 0, pl.ds(start, half)] = (-(wave_real * real - wave_imag * imag)).astype(jnp.bfloat16)
            out[1, 0, pl.ds(start, half)] = (-(wave_real * imag + wave_imag * real)).astype(jnp.bfloat16)

    smem, vmem = pl.BlockSpec(memory_space=pltpu.SMEM), pl.BlockSpec(memory_space=pltpu.VMEM)
    return pl.pallas_call(
        kernel,
        grid=(1,),
        out_shape=jax.ShapeDtypeStruct((2, 2, 2 * half, lanes), jnp.bfloat16),
        in_specs=[smem, smem] + [vmem] * 4 + [pl.BlockSpec(memory_space=pl.ANY)] * len(prior),
        out_specs=pl.BlockSpec((2, 1, 2 * half, lanes), lambda i: (0, g, 0, 0)),
        input_output_aliases={6: 0} if prior else {},
        cost_estimate=pl.CostEstimate(flops=8 * 2 * half * lanes, bytes_accessed=1 << 20, transcendentals=0),
    )(odd, wavelet, *blocks, *prior)


def step(spectra, wavelet):
    zq, core, x = lax.axis_index("zq"), lax.axis_index("core"), lax.axis_index("x")
    y, zh = lax.axis_index("y"), lax.axis_index("zh")
    place = jnp.stack([core, zh, zq, y]).astype(jnp.int32)
    rows, _ = spectra.shape[2:]
    window = NOUT * rows // 512
    half = window // 2
    first = core == 0

    def ordered(block):
        return block.reshape((2, 2, 4, 2) + block.shape[2:])

    passed = swap_core(lax.dynamic_slice_in_dim(spectra, (1 - core) * half, half, 2))
    a = ordered(jnp.where(first, spectra[:, :, :half], passed)).transpose(2, 1, 3, 0, 4, 5)
    a = a.reshape((8, 2, 2) + a.shape[4:])
    b = jnp.where(first, jnp.concatenate([spectra[:, :, window:], passed], 2), spectra[:, :, half:])
    b = [ordered(b)[:, :, :, g].transpose(2, 1, 0, 3, 4) for g in range(2)]
    b = [b[g].reshape((8, 2) + b[g].shape[3:]) for g in range(2)]
    b = lax.optimization_barrier(b)

    def exchange(block):
        return lax.all_to_all(block, ("x", "zr"), split_axis=0, concat_axis=0, tiled=True)

    a_own = exchange(a)
    a_own, *b = lax.optimization_barrier((a_own, *b))
    a_peer = swap_core(a_own)
    b_own, b_peer = [], []
    for g in range(2):
        b_own.append(exchange(b[g]))
        b_peer.append(swap_core(b_own[g]))

    def turn(g):
        shots = a_own.reshape((4, 2) + a_own.shape[1:])[:, 0, g]
        near, far = shots[:2], shots[2:]
        across = send(near, lambda q, r, c, x, y, h: (0, r, c, x, y, 1 - h) if q == 0 else None)
        up = send(far, lambda q, r, c, x, y, h: (1, r, c, x, y, h) if q == 0 else None)
        down = send(far, lambda q, r, c, x, y, h: (1, r, c, x, y, 1 - h) if q == 0 else None)
        mine, across, up, down = lax.optimization_barrier((near, across, up, down))
        pieces = jnp.stack([jnp.where(zq == 0, mine, up), jnp.where(zq == 0, across, down)])
        plus, minus, two = (
            lax.ppermute(pieces, "y", [(i, (i + s) % 4) for i in range(4)]) for s in (1, 3, 2)
        )
        return pieces, plus, two, minus

    turned = [turn(g) for g in range(2)]

    def homeward(blocks):
        moved_on = []
        for t, block in enumerate(blocks):
            moved_on.append(
                send(block, lambda q, r, c, x, y, h: (r, x // 2, x % 2, (2 * q + c) ^ t, y, h))
            )
        return moved_on

    blocks = []
    for g in range(2):
        partial = contract(g, place, turned[g], a_own, a_peer, b_own[g], b_peer[g])
        blocks.append(homeward(partial))
    odd = jnp.stack([x % 2]).astype(jnp.int32)
    early = finish(0, odd, wavelet, blocks[0])
    return finish(1, odd, wavelet, blocks[1], (early,))


def solution(mesh):
    fine = Mesh(mesh.devices.reshape(SIZES), AXES)
    freq, col = AXES[:3], AXES[3:]
    return jax.shard_map(
        step,
        mesh=fine,
        in_specs=(P(None, None, freq, col), P(None, freq)),
        out_specs=P(None, freq, None, col),
        check_vma=False,
    )
```

```python
import jax
import jax.numpy as jnp
from jax import lax
from jax.experimental import pallas as pl
from jax.experimental.pallas import tpu as pltpu
from jax.sharding import Mesh, PartitionSpec as P


NOUT = 384
AXES = ("zq", "zr", "core", "x", "y", "zh")
SIZES = (2, 2, 2, 4, 4, 2)


def coordinates():
    out = [()]
    for size in SIZES:
        out = [c + (i,) for c in out for i in range(size)]
    return out


def flat(c):
    index = 0
    for i, size in zip(c, SIZES):
        index = index * size + i
    return index


def moved(target):
    pairs = []
    for c in coordinates():
        t = target(*c)
        if t is not None:
            pairs.append((flat(c), flat(t)))
    return pairs


def send(value, target):
    return lax.ppermute(value, AXES, moved(target))


def swap_core(value):
    return lax.ppermute(value, "core", [(0, 1), (1, 0)])


def contract(place, turned, a_own, a_peer, b_own, b_peer):
    half, lanes = turned[0].shape[-2:]
    depth = 16 * lanes

    def kernel(place_ref, u0, u1, u2, u3, ao_ref, ap_ref, bo_ref, bp_ref, o0, o1, o2, o3, left):
        core, zh, zq, y = place_ref[0], place_ref[1], place_ref[2], place_ref[3]
        for step, u_ref in enumerate((u0, u1, u2, u3)):
            ys = (y + 4 - step) % 4
            for xl in range(2):
                for piece in range(2):
                    start = pl.multiple_of(((xl * 4 + ys) * 2 + (piece ^ zh)) * lanes, lanes)
                    for part in range(2):
                        left[part * half : (part + 1) * half, pl.ds(start, lanes)] = u_ref[piece, xl, part]

        first = core == 0
        for t, out in enumerate((o0, o1, o2, o3)):
            x = (2 * zq + core) ^ t
            rows = []
            for zr in range(2):
                i = 2 * x + zr
                parts = []
                for part in range(2):
                    ao, ap = ao_ref[i, part], ap_ref[i, part]
                    bo, bp = bo_ref[i, part], bp_ref[i, part]
                    parts.append(
                        jnp.concatenate(
                            [
                                jnp.where(first, ao, ap),
                                jnp.where(first, ap, ao),
                                jnp.where(first, bo, bp),
                                jnp.where(first, bp, bo),
                            ],
                            0,
                        )
                    )
                rows.append(jnp.concatenate(parts, 1))
            right = jnp.concatenate(rows, 0)
            both = jnp.dot(left[...], right, preferred_element_type=jnp.float32)
            out[0] = both[:half, :lanes] - both[half:, lanes:]
            out[1] = both[:half, lanes:] + both[half:, :lanes]

    vmem = pl.BlockSpec(memory_space=pltpu.VMEM)
    result = jax.ShapeDtypeStruct((2, half, lanes), jnp.float32)
    return pl.pallas_call(
        kernel,
        out_shape=(result,) * 4,
        in_specs=[pl.BlockSpec(memory_space=pltpu.SMEM)] + [vmem] * 8,
        out_specs=(vmem,) * 4,
        scratch_shapes=[pltpu.VMEM((2 * half, depth), jnp.bfloat16)],
        cost_estimate=pl.CostEstimate(
            flops=2 * 2 * half * depth * 8 * lanes, bytes_accessed=7 << 20, transcendentals=0
        ),
        compiler_params=pltpu.CompilerParams(vmem_limit_bytes=40 << 20),
    )(place, *turned, a_own, a_peer, b_own, b_peer)


def finish(g, odd, wavelet, blocks, prior=()):
    half, lanes = blocks[0].shape[1:]

    def kernel(odd_ref, wave_ref, *refs):
        wave_real, wave_imag = wave_ref[0, g], wave_ref[1, g]
        out = refs[-1]
        for t in range(2):
            start = pl.multiple_of((odd_ref[0] ^ t) * half, half)
            one, two = refs[t], refs[t + 2]
            real, imag = one[0] + two[0], one[1] + two[1]
            out[0, 0, pl.ds(start, half)] = (-(wave_real * real - wave_imag * imag)).astype(jnp.bfloat16)
            out[1, 0, pl.ds(start, half)] = (-(wave_real * imag + wave_imag * real)).astype(jnp.bfloat16)

    smem, vmem = pl.BlockSpec(memory_space=pltpu.SMEM), pl.BlockSpec(memory_space=pltpu.VMEM)
    return pl.pallas_call(
        kernel,
        grid=(1,),
        out_shape=jax.ShapeDtypeStruct((2, 2, 2 * half, lanes), jnp.bfloat16),
        in_specs=[smem, smem] + [vmem] * 4 + [pl.BlockSpec(memory_space=pl.ANY)] * len(prior),
        out_specs=pl.BlockSpec((2, 1, 2 * half, lanes), lambda i: (0, g, 0, 0)),
        input_output_aliases={6: 0} if prior else {},
        cost_estimate=pl.CostEstimate(flops=8 * 2 * half * lanes, bytes_accessed=1 << 20, transcendentals=0),
    )(odd, wavelet, *blocks, *prior)


def step(spectra, wavelet):
    zq, core, x = lax.axis_index("zq"), lax.axis_index("core"), lax.axis_index("x")
    y, zh = lax.axis_index("y"), lax.axis_index("zh")
    place = jnp.stack([core, zh, zq, y]).astype(jnp.int32)
    rows, _ = spectra.shape[2:]
    window = NOUT * rows // 512
    half = window // 2
    first = core == 0

    def ordered(block):
        return block.reshape((2, 2, 4, 2) + block.shape[2:])

    passed = swap_core(lax.dynamic_slice_in_dim(spectra, (1 - core) * half, half, 2))
    a = ordered(jnp.where(first, spectra[:, :, :half], passed)).transpose(3, 2, 1, 0, 4, 5)
    a = a.reshape((2, 8, 2) + a.shape[4:])
    b = jnp.where(first, jnp.concatenate([spectra[:, :, window:], passed], 2), spectra[:, :, half:])
    b = [ordered(b)[:, :, :, g].transpose(2, 1, 0, 3, 4) for g in range(2)]
    b = [b[g].reshape((8, 2) + b[g].shape[3:]) for g in range(2)]
    b = lax.optimization_barrier(b)

    def exchange(block):
        return lax.all_to_all(block, ("x", "zr"), split_axis=0, concat_axis=0, tiled=True)

    a_own, a_peer = [], []
    for g in range(2):
        a_own.append(exchange(a[g]))
    a_sent = list(a_own)
    *a_own, b[0], b[1] = lax.optimization_barrier((*a_own, *b))
    for g in range(2):
        a_peer.append(swap_core(a_own[g]))
    b_own, b_peer = [], []
    for g in range(2):
        b_own.append(exchange(b[g]))
        b_peer.append(swap_core(b_own[g]))

    def turn(g):
        shots = a_sent[g].reshape((4, 2) + a_sent[g].shape[1:])[:, 0]
        near, far = shots[:2], shots[2:]
        across = send(near, lambda q, r, c, x, y, h: (0, r, c, x, y, 1 - h) if q == 0 else None)
        up = send(far, lambda q, r, c, x, y, h: (1, r, c, x, y, h) if q == 0 else None)
        down = send(far, lambda q, r, c, x, y, h: (1, r, c, x, y, 1 - h) if q == 0 else None)
        mine, across, up, down = lax.optimization_barrier((near, across, up, down))
        pieces = jnp.stack([jnp.where(zq == 0, mine, up), jnp.where(zq == 0, across, down)])
        plus, minus, two = (
            lax.ppermute(pieces, "y", [(i, (i + s) % 4) for i in range(4)]) for s in (1, 3, 2)
        )
        return pieces, plus, two, minus

    turned = [turn(g) for g in range(2)]

    def homeward(blocks):
        return [
            send(
                block,
                lambda q, r, c, x, y, h: (r, x // 2, x % 2, (2 * q + c) ^ t, y, h),
            )
            for t, block in enumerate(blocks)
        ]

    blocks = []
    for g in range(2):
        partial = contract(place, turned[g], a_own[g], a_peer[g], b_own[g], b_peer[g])
        blocks.append(homeward(partial))
    odd = jnp.stack([x % 2]).astype(jnp.int32)
    early = finish(0, odd, wavelet, blocks[0])
    return finish(1, odd, wavelet, blocks[1], (early,))


def solution(mesh):
    fine = Mesh(mesh.devices.reshape(SIZES), AXES)
    freq, col = AXES[:3], AXES[3:]
    return jax.shard_map(
        step,
        mesh=fine,
        in_specs=(P(None, None, freq, col), P(None, freq)),
        out_specs=P(None, freq, None, col),
        check_vma=False,
    )
```

```python
import jax
import jax.numpy as jnp
from jax import lax
from jax.experimental import pallas as pl
from jax.experimental.pallas import tpu as pltpu
from jax.sharding import Mesh, PartitionSpec as P


NOUT = 384
AXES = ("zq", "zr", "core", "x", "y", "zh")
SIZES = (2, 2, 2, 4, 4, 2)


def coordinates():
    out = [()]
    for size in SIZES:
        out = [c + (i,) for c in out for i in range(size)]
    return out


def flat(c):
    index = 0
    for i, size in zip(c, SIZES):
        index = index * size + i
    return index


def moved(target):
    pairs = []
    for c in coordinates():
        t = target(*c)
        if t is not None:
            pairs.append((flat(c), flat(t)))
    return pairs


def send(value, target):
    return lax.ppermute(value, AXES, moved(target))


def swap_core(value):
    return lax.ppermute(value, "core", [(0, 1), (1, 0)])


def contract(g, place, turned, a_own, a_peer, b_own, b_peer):
    half, lanes = turned[0].shape[-2:]
    depth = 16 * lanes

    def kernel(place_ref, u0, u1, u2, u3, ao_ref, ap_ref, bo_ref, bp_ref, o0, o1, o2, o3, left):
        core, zh, zq, y = place_ref[0], place_ref[1], place_ref[2], place_ref[3]
        for step, u_ref in enumerate((u0, u1, u2, u3)):
            ys = (y + 4 - step) % 4
            for xl in range(2):
                for piece in range(2):
                    start = pl.multiple_of(((xl * 4 + ys) * 2 + (piece ^ zh)) * lanes, lanes)
                    for part in range(2):
                        left[part * half : (part + 1) * half, pl.ds(start, lanes)] = u_ref[piece, xl, part]

        first = core == 0
        for t, out in enumerate((o0, o1, o2, o3)):
            x = (2 * zq + core) ^ t
            rows = []
            for zr in range(2):
                i = 2 * x + zr
                parts = []
                for part in range(2):
                    ao, ap = ao_ref[i, g, part], ap_ref[i, g, part]
                    bo, bp = bo_ref[i, part], bp_ref[i, part]
                    parts.append(
                        jnp.concatenate(
                            [
                                jnp.where(first, ao, ap),
                                jnp.where(first, ap, ao),
                                jnp.where(first, bo, bp),
                                jnp.where(first, bp, bo),
                            ],
                            0,
                        )
                    )
                rows.append(jnp.concatenate(parts, 1))
            right = jnp.concatenate(rows, 0)
            both = jnp.dot(left[...], right, preferred_element_type=jnp.float32)
            out[0] = both[:half, :lanes] - both[half:, lanes:]
            out[1] = both[:half, lanes:] + both[half:, :lanes]

    vmem = pl.BlockSpec(memory_space=pltpu.VMEM)
    result = jax.ShapeDtypeStruct((2, half, lanes), jnp.float32)
    return pl.pallas_call(
        kernel,
        out_shape=(result,) * 4,
        in_specs=[pl.BlockSpec(memory_space=pltpu.SMEM)] + [vmem] * 8,
        out_specs=(vmem,) * 4,
        scratch_shapes=[pltpu.VMEM((2 * half, depth), jnp.bfloat16)],
        cost_estimate=pl.CostEstimate(
            flops=2 * 2 * half * depth * 8 * lanes, bytes_accessed=7 << 20, transcendentals=0
        ),
        compiler_params=pltpu.CompilerParams(vmem_limit_bytes=40 << 20),
    )(place, *turned, a_own, a_peer, b_own, b_peer)


def finish(g, odd, wavelet, blocks, prior=()):
    half, lanes = blocks[0].shape[1:]

    def kernel(odd_ref, wave_ref, *refs):
        wave_real, wave_imag = wave_ref[0, g], wave_ref[1, g]
        out = refs[-1]
        for t in range(2):
            start = pl.multiple_of((odd_ref[0] ^ t) * half, half)
            one, two = refs[t], refs[t + 2]
            real, imag = one[0] + two[0], one[1] + two[1]
            out[0, 0, pl.ds(start, half)] = (-(wave_real * real - wave_imag * imag)).astype(jnp.bfloat16)
            out[1, 0, pl.ds(start, half)] = (-(wave_real * imag + wave_imag * real)).astype(jnp.bfloat16)

    smem, vmem = pl.BlockSpec(memory_space=pltpu.SMEM), pl.BlockSpec(memory_space=pltpu.VMEM)
    return pl.pallas_call(
        kernel,
        grid=(1,),
        out_shape=jax.ShapeDtypeStruct((2, 2, 2 * half, lanes), jnp.bfloat16),
        in_specs=[smem, smem] + [vmem] * 4 + [pl.BlockSpec(memory_space=pl.ANY)] * len(prior),
        out_specs=pl.BlockSpec((2, 1, 2 * half, lanes), lambda i: (0, g, 0, 0)),
        input_output_aliases={6: 0} if prior else {},
        cost_estimate=pl.CostEstimate(flops=8 * 2 * half * lanes, bytes_accessed=1 << 20, transcendentals=0),
    )(odd, wavelet, *blocks, *prior)


def step(spectra, wavelet):
    zq, core, x = lax.axis_index("zq"), lax.axis_index("core"), lax.axis_index("x")
    y, zh = lax.axis_index("y"), lax.axis_index("zh")
    place = jnp.stack([core, zh, zq, y]).astype(jnp.int32)
    rows, _ = spectra.shape[2:]
    window = NOUT * rows // 512
    half = window // 2
    first = core == 0

    def ordered(block):
        return block.reshape((2, 2, 4, 2) + block.shape[2:])

    passed = swap_core(lax.dynamic_slice_in_dim(spectra, (1 - core) * half, half, 2))
    a = ordered(jnp.where(first, spectra[:, :, :half], passed)).transpose(2, 1, 3, 0, 4, 5)
    a = a.reshape((8, 2, 2) + a.shape[4:])
    b = jnp.where(first, jnp.concatenate([spectra[:, :, window:], passed], 2), spectra[:, :, half:])
    b = [ordered(b)[:, :, :, g].transpose(2, 1, 0, 3, 4) for g in range(2)]
    b = [b[g].reshape((8, 2) + b[g].shape[3:]) for g in range(2)]
    b = lax.optimization_barrier(b)

    def exchange(block):
        return lax.all_to_all(block, ("x", "zr"), split_axis=0, concat_axis=0, tiled=True)

    a_own = exchange(a)
    a_own, *b = lax.optimization_barrier((a_own, *b))
    a_peer = swap_core(a_own)
    b_own, b_peer = [], []
    for g in range(2):
        b_own.append(exchange(b[g]))
        b_peer.append(swap_core(b_own[g]))

    def turn(g):
        shots = a_own.reshape((4, 2) + a_own.shape[1:])[:, 0, g]
        near, far = shots[:2], shots[2:]
        across = send(near, lambda q, r, c, x, y, h: (0, r, c, x, y, 1 - h) if q == 0 else None)
        up = send(far, lambda q, r, c, x, y, h: (1, r, c, x, y, h) if q == 0 else None)
        down = send(far, lambda q, r, c, x, y, h: (1, r, c, x, y, 1 - h) if q == 0 else None)
        mine, across, up, down = lax.optimization_barrier((near, across, up, down))
        pieces = jnp.stack([jnp.where(zq == 0, mine, up), jnp.where(zq == 0, across, down)])
        plus, minus, two = (
            lax.ppermute(pieces, "y", [(i, (i + s) % 4) for i in range(4)]) for s in (1, 3, 2)
        )
        return pieces, plus, two, minus

    turned = [turn(g) for g in range(2)]

    def homeward(blocks):
        return [
            send(
                block,
                lambda q, r, c, x, y, h: (r, x // 2, x % 2, (2 * q + c) ^ t, y, h),
            )
            for t, block in enumerate(blocks)
        ]

    blocks = []
    for g in range(2):
        partial = contract(g, place, turned[g], a_own, a_peer, b_own[g], b_peer[g])
        blocks.append(homeward(partial))
    odd = jnp.stack([x % 2]).astype(jnp.int32)
    early = finish(0, odd, wavelet, blocks[0])
    return finish(1, odd, wavelet, blocks[1], (early,))


def solution(mesh):
    fine = Mesh(mesh.devices.reshape(SIZES), AXES)
    freq, col = AXES[:3], AXES[3:]
    return jax.shard_map(
        step,
        mesh=fine,
        in_specs=(P(None, None, freq, col), P(None, freq)),
        out_specs=P(None, freq, None, col),
        check_vma=False,
    )
```
